32 devices in a mesh: dp: 8 (over y, x, core), tensor: 4 (over z).
Axes of the slice: x: 2, y: 2, z: 4, core: 2. Of those that a mesh axis runs over, the one named last changes fastest.
Arguments:
- tokens: bfloat16 [580, 32, 1024], P('tensor', 'dp'), may hold values from -6 to 6
- attn_gain: bfloat16 [1024], P('dp'), may hold values from 0.099609375 to 1.8984375
- attn_shift: bfloat16 [1024], P('dp'), may hold values from -3 to 3
- qkv_weight: bfloat16 [1024, 3, 1024], P('dp', None, 'tensor'), may hold values from -0.1875 to 0.1875
- query_value_bias: bfloat16 [2, 16, 64], P(None, 'tensor', 'dp'), may hold values from -3 to 3
- proj_weight: bfloat16 [1024, 1024], P('tensor', 'dp'), may hold values from -3 to 3
- proj_bias: bfloat16 [1024], P('dp'), may hold values from -3 to 3
- mlp_gain: bfloat16 [1024], P('dp'), may hold values from 0.099609375 to 1.8984375
- mlp_shift: bfloat16 [1024], P('dp'), may hold values from -3 to 3
- expand_weight: bfloat16 [1024, 4096], P('dp', 'tensor'), may hold values from -0.1875 to 0.1875
- expand_bias: bfloat16 [4, 1024], P('tensor', 'dp'), may hold values from -3 to 3
- reduce_weight: bfloat16 [4096, 1024], P('tensor', 'dp'), may hold values from -0.25 to 0.25
- reduce_bias: bfloat16 [1024], P('dp'), may hold values from -3 to 3
- key_mask: int32 [32, 580], P('dp'), may hold values from 0 to 1, as said below
- cotangent: bfloat16 [580, 32, 1024], P('tensor', 'dp'), may hold values from -6 to 6
Outputs:
- block_output: bfloat16 [580, 32, 1024], P('tensor', 'dp')
- tokens_grad: bfloat16 [580, 32, 1024], P('tensor', 'dp')
- attn_gain_grad: float32 [1024], P('dp')
- attn_shift_grad: float32 [1024], P('dp')
- qkv_weight_grad: float32 [1024, 3, 1024], P('dp', None, 'tensor')
- query_value_bias_grad: float32 [2, 16, 64], P(None, 'tensor', 'dp')
- proj_weight_grad: float32 [1024, 1024], P('tensor', 'dp')
- proj_bias_grad: float32 [1024], P('dp')
- mlp_gain_grad: float32 [1024], P('dp')
- mlp_shift_grad: float32 [1024], P('dp')
- expand_weight_grad: float32 [1024, 4096], P('dp', 'tensor')
- expand_bias_grad: float32 [4, 1024], P('tensor', 'dp')
- reduce_weight_grad: float32 [4096, 1024], P('tensor', 'dp')
- reduce_bias_grad: float32 [1024], P('dp')
The draws below stay inside these ranges and needn't reach their ends.
Inputs may be any that keep to these rules, and one draw needn't show every extreme that they name: `key_mask`: each image's row is 1 on its first positions and 0 after them; every image has at least 288 ones and at most 577, and some image has exactly 577.
All inputs are finite; a program needn't handle non-finite values.
Results may differ from the reference program's by a relative error of at most 0.013.
Values may be sent and summed in bfloat16 or wider, within the bound.
No kernel may reach another device: no remote copies, remote signals or barrier semaphores. Data moves between devices by JAX's collectives and lax.ppermute only.
A program may use at most 192 MiB of HBM per device.

```python
import jax
import jax.numpy as jnp
from jax import lax

D = 1024
HEADS = 16
HD = 64
FF = 4096
LEN = 577
S = 580
IMAGES = 32
N_TENSOR = 4


def draw_key_mask(key, part):
    length_key = jax.random.fold_in(key, 21)
    chosen_key = jax.random.fold_in(key, 22)
    lengths = jax.random.randint(length_key, (IMAGES,), LEN // 2, LEN + 1)
    chosen = jax.random.randint(chosen_key, (), 0, IMAGES)
    lengths = jnp.where(jnp.arange(IMAGES) == chosen, LEN, lengths)
    positions = jnp.arange(S)
    return (positions[None, :] < lengths[:, None]).astype(jnp.int32)


def shard_levels(key, dims, cuts, least, top_value):
    factor_of = 1.0
    for dim, parts in cuts:
        steps = jax.random.uniform(jax.random.fold_in(jax.random.fold_in(key, 6), dim), (parts,), jnp.float32, least / len(cuts), top_value / len(cuts))
        factor_of = factor_of * jnp.repeat(jnp.exp(steps), dims[dim] // parts).reshape((-1,) + (1,) * (len(dims) - 1 - dim))
    return factor_of


def gaussian(key, shape, deviation, bound, pieces=(), kind=jnp.bfloat16):
    drawn = jax.random.normal(key, shape, jnp.float32) * deviation
    if len(pieces) > 0:
        drawn = shard_levels(key, shape, pieces, -0.22, 0.18) * drawn
    return jnp.clip(drawn, min=-bound, max=bound).astype(kind)


def setup_inputs(seed: int = 0) -> dict:
    streams_of = jax.random.split(jax.random.key(seed), 16)
    tokens = gaussian(streams_of[0], (S, IMAGES, D), 1.0, 6.0, ((0, 4), (1, 8)))
    attn_gain = jnp.clip(1.0 + 0.18 * jax.random.normal(streams_of[1], (D,), jnp.float32), 0.099609375, 1.8984375).astype(jnp.bfloat16)
    attn_shift = gaussian(streams_of[2], (D,), 0.5, 3.0, ((0, 8),))
    qkv_weight = gaussian(streams_of[3], (D, 3, D), D ** -0.5, 0.1875, ((0, 8), (2, 4)))
    query_value_bias = gaussian(streams_of[4], (2, HEADS, HD), 0.5, 3.0, ((1, 4), (2, 8)))
    proj_weight = gaussian(streams_of[5], (D, D), (max(D // 256, 1)) ** -0.5, 3.0, ((0, 4), (1, 8)))
    proj_bias = gaussian(streams_of[6], (D,), 0.5, 3.0, ((0, 8),))
    mlp_gain = jnp.clip(1.0 + 0.18 * jax.random.normal(streams_of[7], (D,), jnp.float32), 0.099609375, 1.8984375).astype(jnp.bfloat16)
    mlp_shift = gaussian(streams_of[8], (D,), 0.5, 3.0, ((0, 8),))
    expand_weight = gaussian(streams_of[9], (D, FF), D ** -0.5, 0.1875, ((0, 8), (1, 4)))
    expand_bias = gaussian(streams_of[10], (N_TENSOR, FF // N_TENSOR), 0.5, 3.0, ((0, 4), (1, 8)))
    reduce_weight = gaussian(streams_of[11], (FF, D), (FF // 8) ** -0.5, 0.25, ((0, 4), (1, 8)))
    reduce_bias = gaussian(streams_of[12], (D,), 0.5, 3.0, ((0, 8),))
    key_mask = draw_key_mask(jax.random.fold_in(streams_of[15], 71), 0)
    cotangent = gaussian(streams_of[14], (S, IMAGES, D), 1.0, 6.0, ((0, 4), (1, 8)))
    return {"tokens": tokens, "attn_gain": attn_gain, "attn_shift": attn_shift, "qkv_weight": qkv_weight, "query_value_bias": query_value_bias, "proj_weight": proj_weight, "proj_bias": proj_bias, "mlp_gain": mlp_gain, "mlp_shift": mlp_shift, "expand_weight": expand_weight, "expand_bias": expand_bias, "reduce_weight": reduce_weight, "reduce_bias": reduce_bias, "key_mask": key_mask, "cotangent": cotangent}


EPSILON = 1e-06
NEG_FILL = -1e+30
HIGHEST = lax.Precision.HIGHEST

@jax.custom_vjp
def low(v):
    return lax.optimization_barrier(v.astype(jnp.bfloat16)).astype(jnp.float32)

@jax.custom_vjp
def low_back(v):
    return v

def low_keep(v):
    return (low(v), None)

def low_pass(kept, grad):
    return (grad,)

def back_keep(v):
    return (v, None)

def back_low(kept, grad):
    return (low(grad),)
low.defvjp(low_keep, low_pass)
low_back.defvjp(back_keep, back_low)

def layer_norm(row_values, gain_vector, shift_vector):
    average = lax.optimization_barrier(jnp.mean(row_values, axis=-1, keepdims=True))
    centered = row_values - average
    variance = lax.optimization_barrier(jnp.mean(centered * centered, axis=-1, keepdims=True))
    return centered * lax.rsqrt(variance + EPSILON) * gain_vector + shift_vector

def block_forward(parameters, tokens, key_valid):
    attn_gain, attn_shift, qkv_weight, query_value_bias, proj_weight, proj_bias, mlp_gain, mlp_shift, expand_weight, expand_bias, reduce_weight, reduce_bias = parameters
    length = tokens.shape[0]
    images = tokens.shape[1]
    features = tokens.shape[2]
    normed = low(layer_norm(tokens, attn_gain, attn_shift))
    bias_rows = query_value_bias.reshape(2, features)
    bias_three = jnp.stack([bias_rows[0], jnp.zeros_like(bias_rows[0]), bias_rows[1]])
    projected = jnp.einsum('sbd,dce->sbce', normed, qkv_weight, precision=HIGHEST) + bias_three
    projected = low(low_back(projected))
    split_heads = projected.reshape(length, images, 3, HEADS, HD)
    queries = split_heads[:, :, 0]
    key_rows = split_heads[:, :, 1]
    values = split_heads[:, :, 2]
    raw_scores = jnp.einsum('qbhe,kbhe->bhqk', queries, key_rows, precision=HIGHEST) * HD ** (-0.5)
    raw_scores = low_back(raw_scores)
    masked = jnp.where(key_valid[:, None, None, :], raw_scores, NEG_FILL)
    highest = lax.optimization_barrier(jnp.max(masked, axis=-1, keepdims=True))
    expanded = jnp.exp(masked - highest)
    attention = low(expanded / lax.optimization_barrier(jnp.sum(expanded, axis=-1, keepdims=True)))
    attended = jnp.einsum('bhqk,kbhe->qbhe', attention, values, precision=HIGHEST)
    attended = low(low_back(attended.reshape(length, images, features)))
    branch = low_back(jnp.einsum('sbe,ed->sbd', attended, proj_weight, precision=HIGHEST))
    middle = tokens + branch + proj_bias
    normed_two = low(layer_norm(middle, mlp_gain, mlp_shift))
    before = jnp.einsum('sbd,df->sbf', normed_two, expand_weight, precision=HIGHEST) + expand_bias.reshape(-1)
    before = low_back(before)
    hidden = low(jax.nn.gelu(before, approximate=False))
    mlp_branch = low_back(jnp.einsum('sbf,fd->sbd', hidden, reduce_weight, precision=HIGHEST))
    return middle + mlp_branch + reduce_bias

def reference(tokens, attn_gain, attn_shift, qkv_weight, query_value_bias, proj_weight, proj_bias, mlp_gain, mlp_shift, expand_weight, expand_bias, reduce_weight, reduce_bias, key_mask, cotangent):
    parameters = tuple((parameter.astype(jnp.float32) for parameter in (attn_gain, attn_shift, qkv_weight, query_value_bias, proj_weight, proj_bias, mlp_gain, mlp_shift, expand_weight, expand_bias, reduce_weight, reduce_bias)))
    length = tokens.shape[0]
    features = tokens.shape[2]
    group_size = max([candidate for candidate in range(1, IMAGES + 1) if IMAGES % candidate == 0 and candidate * S <= 4096] + [1])
    group_count = IMAGES // group_size
    token_groups = jnp.moveaxis(tokens.astype(jnp.float32).reshape(length, group_count, group_size, features), 1, 0)
    grad_groups = jnp.moveaxis(cotangent.astype(jnp.float32).reshape(length, group_count, group_size, features), 1, 0)
    mask_groups = key_mask.reshape(group_count, group_size, length) > 0
    zero_grads = jax.tree.map(jnp.zeros_like, parameters)

    def one_group(totals_so_far, inputs):
        token_rows, grad_rows, key_valid = inputs
        output, pullback = jax.vjp(lambda weights, row_block: block_forward(weights, row_block, key_valid), parameters, token_rows)
        param_grads, token_grad = pullback(grad_rows)
        updated = jax.tree.map(jnp.add, totals_so_far, param_grads)
        return (updated, (output.astype(jnp.bfloat16), token_grad.astype(jnp.bfloat16)))
    totals, (outputs, token_grads) = lax.scan(one_group, zero_grads, (token_groups, grad_groups, mask_groups))
    block_output = jnp.moveaxis(outputs, 0, 1).reshape(length, IMAGES, features)
    tokens_grad = jnp.moveaxis(token_grads, 0, 1).reshape(length, IMAGES, features)
    return (block_output, tokens_grad, totals[0], totals[1], totals[2], totals[3], totals[4], totals[5], totals[6], totals[7], totals[8], totals[9], totals[10], totals[11])
```

```python
from functools import partial

import jax
import jax.numpy as jnp
from jax import lax
from jax.sharding import PartitionSpec as P

HD = 64
EPSILON = 1e-06
NEG_FILL = -1e30
LOW = jnp.bfloat16
FULL = jnp.float32
ORDER = (0, 2, 4, 6, 1, 3, 5, 7)
SMALL_ROWS = 16


def norm_parts(row_values):
    average = jnp.mean(row_values, axis=-1, keepdims=True)
    centered = row_values - average
    variance = jnp.mean(centered * centered, axis=-1, keepdims=True)
    scaling = lax.rsqrt(variance + EPSILON)
    return (centered * scaling, scaling)


def norm_back(grad_output, normal, scaling, gain_vector):
    grad_normal = grad_output * gain_vector
    first_mean = jnp.mean(grad_normal, axis=-1, keepdims=True)
    second_mean = jnp.mean(grad_normal * normal, axis=-1, keepdims=True)
    return scaling * (grad_normal - first_mean - normal * second_mean)


def dot(left, right, contract, kind=FULL):
    return lax.dot_general(
        left, right, (contract, ((), ())), preferred_element_type=kind
    )


def masked_scores(queries, key_rows, key_valid):
    scores = jnp.einsum(
        "qhe,khe->hqk", queries, key_rows, preferred_element_type=FULL
    ) * HD ** (-0.5)
    return jnp.where(key_valid[None, None, :], scores, NEG_FILL)


def attend_heads(queries, key_rows, values, key_valid):
    scores = masked_scores(queries, key_rows, key_valid)
    highest = jnp.max(scores, axis=-1, keepdims=True)
    expanded = jnp.exp(scores - highest)
    totals = jnp.sum(expanded, axis=-1, keepdims=True)
    attention = (expanded / totals).astype(LOW)
    attended = jnp.einsum("hqk,khe->qhe", attention, values, preferred_element_type=FULL)
    return (attended.astype(LOW), highest[..., 0] + jnp.log(totals[..., 0]))


def attend_back(queries, key_rows, values, grad_att, log_total, key_valid):
    scores = masked_scores(queries, key_rows, key_valid)
    attention = jnp.exp(scores - log_total[..., None])
    grad_values = jnp.einsum(
        "hqk,qhe->khe", attention.astype(LOW), grad_att, preferred_element_type=FULL
    )
    grad_probs = jnp.einsum("qhe,khe->hqk", grad_att, values, preferred_element_type=FULL)
    inner_sum = jnp.sum(attention * grad_probs, axis=-1, keepdims=True)
    grad_scores = (attention * (grad_probs - inner_sum)).astype(LOW)
    grad_queries = jnp.einsum(
        "hqk,khe->qhe", grad_scores, key_rows, preferred_element_type=FULL
    ) * HD ** (-0.5)
    grad_keys = jnp.einsum(
        "hqk,qhe->khe", grad_scores, queries, preferred_element_type=FULL
    ) * HD ** (-0.5)
    return grad_queries, grad_keys, grad_values


class Layout:
    def __init__(self, sizes, images):
        self.dp, self.tensor = sizes["dp"], sizes["tensor"]
        self.images = images
        self.groups = self.tensor // images
        self.near = self.dp == 8
        self.me = lax.axis_index("dp")
        self.place = lax.axis_index("tensor")

    def swap(self, array, bit):
        return lax.ppermute(array, "dp", [(k, k ^ bit) for k in range(self.dp)])

    def swap_tensor(self, array, step):
        return lax.ppermute(array, "tensor", [(k, k ^ step) for k in range(self.tensor)])

    def ordered(self, array, axis):
        if not self.near:
            return array
        width = array.shape[axis] // 8
        return jnp.concatenate(
            [
                lax.dynamic_slice_in_dim(array, (self.me ^ r) * width, width, axis)
                for r in ORDER
            ],
            axis,
        )

    def plain(self, array, axis):
        if not self.near:
            return array
        width = array.shape[axis] // 8
        pieces = []
        for block in range(8):
            r = self.me ^ block
            position = (r & 1) * 4 + (r >> 1)
            pieces.append(lax.dynamic_slice_in_dim(array, position * width, width, axis))
        return jnp.concatenate(pieces, axis)

    def gather(self, shard):
        line = lax.all_gather(shard, "tensor", axis=1, tiled=True)
        if not self.near:
            return list(lax.all_gather(line, "dp", axis=0))
        half = line.shape[0] // 2
        by_x = self.swap(line, 2)
        by_y = self.swap(line, 4)
        top = self.swap(by_y[:half], 2)
        bottom = self.swap(by_x[half:], 4)
        far = jnp.concatenate([top, bottom], 0)
        mine = [line, by_x, by_y, far]
        return mine + [self.swap(block, 1) for block in mine]

    def scatter(self, kept, sent):
        columns = kept.shape[2] // self.tensor
        if not self.near:
            total = lax.psum_scatter(
                jnp.concatenate([kept, sent], 0), "dp", scatter_dimension=0, tiled=True
            )[0]
        else:
            came = self.swap(sent, 1)
            half = kept.shape[1] // 2

            def add(*parts):
                return sum(part.astype(FULL) for part in parts).astype(LOW)

            top = self.swap(add(kept[3, :half], came[3, :half]), 2)
            bottom = self.swap(add(kept[3, half:], came[3, half:]), 4)
            x_block = jnp.concatenate(
                [add(kept[1, :half], came[1, :half]), add(kept[1, half:], came[1, half:], bottom)],
                0,
            )
            y_block = jnp.concatenate(
                [add(kept[2, :half], came[2, :half], top), add(kept[2, half:], came[2, half:])],
                0,
            )
            total = add(kept[0], came[0], self.swap(x_block, 2), self.swap(y_block, 4))
        rows = total.shape[0]
        stacked = total.reshape(rows, self.tensor, columns).transpose(1, 0, 2)
        return lax.psum_scatter(
            stacked, "tensor", scatter_dimension=0, tiled=True
        ).reshape(rows, columns).astype(FULL)

    def to_image(self, array):
        spot = self.place % self.images
        blocks = [lax.dynamic_index_in_dim(array, spot, 1, keepdims=False)]
        for step in range(1, self.images):
            block = lax.dynamic_index_in_dim(array, spot ^ step, 1, keepdims=False)
            blocks.append(self.swap_tensor(block, step))
        return jnp.concatenate(blocks, 0)

    def from_image(self, array):
        spot = self.place % self.images
        rows = array.shape[0] // self.images
        blocks = [array[:rows]]
        for step in range(1, self.images):
            blocks.append(self.swap_tensor(array[step * rows : (step + 1) * rows], step))
        return jnp.stack(
            [self.pick(blocks, spot ^ image) for image in range(self.images)], 1
        )

    def pick(self, blocks, index):
        chosen = blocks[0]
        for k in range(1, len(blocks)):
            chosen = jnp.where(index == k, blocks[k], chosen)
        return chosen

    def halves(self, array):
        parts = [array]
        for group in range(1, self.groups):
            parts.append(self.swap_tensor(array, group * self.images))
        return parts[0] if len(parts) == 1 else jnp.concatenate(parts, 0)

    def halves_back(self, array):
        rows = array.shape[0] // self.groups
        total = array[:rows]
        for group in range(1, self.groups):
            total = total + self.swap_tensor(
                array[group * rows : (group + 1) * rows], group * self.images
            )
        return total

    def valid_keys(self, key_mask):
        rows = key_mask.shape[1] // self.tensor
        mine = lax.dynamic_index_in_dim(
            key_mask, self.place % self.images, 0, keepdims=False
        )
        return (
            jnp.concatenate(
                [
                    lax.dynamic_slice_in_dim(mine, (self.place ^ block) * rows, rows, 0)
                    for block in range(self.tensor)
                ]
            )
            > 0
        )


def shards(
    sizes,
    tokens,
    attn_gain,
    attn_shift,
    qkv_weight,
    query_value_bias,
    proj_weight,
    proj_bias,
    mlp_gain,
    mlp_shift,
    expand_weight,
    expand_bias,
    reduce_weight,
    reduce_bias,
    key_mask,
    cotangent,
):
    lay = Layout(sizes, tokens.shape[1])
    depth = attn_gain.shape[0]
    width = depth * lay.dp
    cut = qkv_weight.shape[2]
    fan = expand_weight.shape[1]
    heads = cut // HD
    slots = query_value_bias.shape[2]

    pair = query_value_bias.reshape(-1)
    small = jnp.concatenate(
        [
            attn_gain,
            attn_shift,
            proj_bias,
            mlp_gain,
            mlp_shift,
            reduce_bias,
            expand_bias.reshape(-1),
            pair,
        ]
    )
    lanes = 4 * cut
    small = jnp.pad(small, (0, SMALL_ROWS * lanes - small.shape[0])).reshape(SMALL_ROWS, lanes)
    first = jnp.concatenate(
        [
            jnp.concatenate([qkv_weight.reshape(depth, 3 * cut), proj_weight.T], 1),
            small,
        ],
        0,
    )
    first_blocks = lay.gather(first)
    expand_blocks = lay.gather(expand_weight)
    reduce_blocks = lay.gather(reduce_weight.T)
    expand_full = jnp.concatenate(expand_blocks, 0)
    reduce_full = jnp.concatenate(reduce_blocks, 0)
    weights_one = jnp.concatenate(
        [block[:depth].reshape(depth, lay.tensor, lanes) for block in first_blocks], 0
    )
    qkv_full = weights_one[:, :, : 3 * cut].reshape(width, -1)
    proj_full = weights_one[:, :, 3 * cut :].reshape(width, -1)
    smalls = jnp.stack(
        [block[depth:].reshape(SMALL_ROWS, lay.tensor, lanes) for block in first_blocks], 0
    ).transpose(0, 2, 1, 3).reshape(lay.dp, lay.tensor, SMALL_ROWS * lanes).astype(FULL)

    def vector(k):
        return smalls[:, 0, k * depth : (k + 1) * depth].reshape(-1)

    gain_one, shift_one, proj_vector, gain_two, shift_two, reduce_vector = (
        vector(k) for k in range(6)
    )
    at = 6 * depth
    count = expand_bias.size
    expand_row = lay.plain(smalls[:, :, at : at + count], 0).transpose(1, 0, 2).reshape(-1)
    pairs = lay.plain(smalls[:, :, at + count : at + count + pair.size], 0)
    pairs = pairs.reshape(lay.dp, lay.tensor, 2, heads, slots).transpose(2, 1, 3, 0, 4)
    pairs = pairs.reshape(2, lay.tensor, cut)
    bias_three = jnp.stack([pairs[0], jnp.zeros_like(pairs[0]), pairs[1]], 1).reshape(-1)

    rows_input = lay.ordered(lay.to_image(tokens), 1).astype(FULL)
    grad_low = lay.ordered(lay.to_image(cotangent), 1)
    key_valid = lay.valid_keys(key_mask)
    normal_one, scale_one = norm_parts(rows_input)
    normed_one = (normal_one * gain_one + shift_one).astype(LOW)
    projected = (dot(normed_one, qkv_full, ((1,), (0,))) + bias_three).astype(LOW)
    length = projected.shape[0]
    split = projected.reshape(length, lay.tensor, 3, heads, HD)
    queries = split[:, :, 0]
    key_all = lay.halves(split[:, :, 1])
    value_all = lay.halves(split[:, :, 2])

    def by_part(array):
        return array.transpose(1, 0, 2, 3)

    attended, log_total = lax.map(
        lambda ops: attend_heads(*ops, key_valid),
        (by_part(queries), by_part(key_all), by_part(value_all)),
    )
    attended_flat = attended.transpose(1, 0, 2, 3).reshape(length, -1)
    middle = rows_input + dot(attended_flat, proj_full, ((1,), (1,))) + proj_vector
    normal_two, scale_two = norm_parts(middle)
    normed_two = (normal_two * gain_two + shift_two).astype(LOW)
    before = dot(normed_two, expand_full, ((1,), (0,))) + expand_row
    hidden, gelu_back = jax.vjp(partial(jax.nn.gelu, approximate=False), before)
    hidden = hidden.astype(LOW)
    mlp_total = dot(hidden, reduce_full, ((1,), (1,)))
    block_output = lay.from_image(
        lay.plain((middle + mlp_total + reduce_vector).astype(LOW), 1)
    )

    half = width // 2

    def weight_grad(left, right):
        sent = dot(left[:, half:], right, ((0,), (0,))).astype(LOW)
        kept = dot(left[:, :half], right, ((0,), (0,))).astype(LOW)
        shape = (lay.dp // 2, depth, -1)
        return kept.reshape(shape), sent.reshape(shape)

    grad_output = grad_low.astype(FULL)
    reduce_bias_grad = jnp.sum(grad_output, axis=0)
    reduce_grad = lay.scatter(*weight_grad(grad_low, hidden)).T
    grad_before = gelu_back(dot(grad_low, reduce_full, ((1,), (0,))))[0].astype(LOW)
    expand_bias_grad = jnp.sum(grad_before, axis=0, dtype=FULL)
    expand_grad = lay.scatter(*weight_grad(normed_two, grad_before))
    grad_normed_two = dot(grad_before, expand_full, ((1,), (1,)))
    mlp_gain_grad = jnp.sum(grad_normed_two * normal_two, axis=0)
    mlp_shift_grad = jnp.sum(grad_normed_two, axis=0)
    grad_middle = grad_output + norm_back(grad_normed_two, normal_two, scale_two, gain_two)
    proj_bias_grad = jnp.sum(grad_middle, axis=0)
    grad_branch = grad_middle.astype(LOW)
    grad_attended = dot(grad_branch, proj_full, ((1,), (0,))).astype(LOW)
    proj_grad = lay.scatter(*weight_grad(grad_branch, attended_flat)).T
    grad_queries, grad_keys, grad_values = lax.map(
        lambda ops: attend_back(*ops, key_valid),
        (
            by_part(queries),
            by_part(key_all),
            by_part(value_all),
            by_part(grad_attended.reshape(length, lay.tensor, heads, HD)),
            log_total,
        ),
    )
    grad_keys = lay.halves_back(grad_keys.transpose(1, 0, 2, 3))
    grad_values = lay.halves_back(grad_values.transpose(1, 0, 2, 3))
    grad_split = jnp.stack([grad_queries.transpose(1, 0, 2, 3), grad_keys, grad_values], 2)
    grad_projected = grad_split.astype(LOW).reshape(length, -1)
    projected_sums = jnp.sum(grad_projected, axis=0, dtype=FULL)
    grad_normed_one = dot(grad_projected, qkv_full, ((1,), (1,)))
    attn_gain_grad = jnp.sum(grad_normed_one * normal_one, axis=0)
    attn_shift_grad = jnp.sum(grad_normed_one, axis=0)
    tokens_grad = (
        grad_middle + norm_back(grad_normed_one, normal_one, scale_one, gain_one)
    ).astype(LOW)
    tokens_grad = lay.from_image(lay.plain(tokens_grad, 1))

    vectors = jnp.stack(
        [
            vector.reshape(lay.dp, 1, depth)
            for vector in (
                attn_gain_grad,
                attn_shift_grad,
                proj_bias_grad,
                mlp_gain_grad,
                mlp_shift_grad,
                reduce_bias_grad,
            )
        ],
        2,
    )
    vectors = jnp.broadcast_to(vectors, (lay.dp, lay.tensor, 6, depth))
    vectors = vectors.reshape(lay.dp, lay.tensor, 6 * depth)
    row_grad = expand_bias_grad.reshape(lay.tensor, lay.dp, count).transpose(1, 0, 2)
    sums = projected_sums.reshape(lay.tensor, 3, heads, lay.dp, slots)
    pair_grad = jnp.stack([sums[:, 0], sums[:, 2]], 1).transpose(3, 0, 1, 2, 4)
    pair_grad = pair_grad.reshape(lay.dp, lay.tensor, -1)
    rest = lay.ordered(jnp.concatenate([row_grad, pair_grad], 2), 0)
    packed = jnp.concatenate([vectors, rest], 2).astype(LOW)
    room = SMALL_ROWS * 3 * cut
    packed = jnp.pad(packed, ((0, 0), (0, 0), (0, room - packed.shape[2])))
    packed = packed.reshape(lay.dp, lay.tensor, SMALL_ROWS, 3 * cut).transpose(0, 2, 1, 3)
    packed = packed.reshape(lay.dp, SMALL_ROWS, -1)
    kept, sent = weight_grad(normed_one, grad_projected)
    kept = jnp.concatenate([kept, packed[: lay.dp // 2]], 1)
    sent = jnp.concatenate([sent, packed[lay.dp // 2 :]], 1)
    last = lay.scatter(kept, sent)
    qkv_grad = last[:depth].reshape(depth, 3, cut)
    flat = last[depth:].reshape(-1)
    vector_grads = flat[:at].reshape(6, depth)
    return (
        block_output,
        tokens_grad,
        vector_grads[0],
        vector_grads[1],
        qkv_grad,
        flat[at + count : at + count + pair.size].reshape(2, heads, slots),
        proj_grad,
        vector_grads[2],
        vector_grads[3],
        vector_grads[4],
        expand_grad,
        flat[at : at + count].reshape(expand_bias.shape),
        reduce_grad,
        vector_grads[5],
    )


def solution(mesh):
    placed = (
        P("tensor", "dp", None),
        P("dp"),
        P("dp"),
        P("dp", None, "tensor"),
        P(None, "tensor", "dp"),
        P("tensor", "dp"),
        P("dp"),
        P("dp"),
        P("dp"),
        P("dp", "tensor"),
        P("tensor", "dp"),
        P("tensor", "dp"),
        P("dp"),
        P("dp", None),
        P("tensor", "dp", None),
    )
    return jax.shard_map(
        partial(shards, dict(mesh.shape)),
        mesh=mesh,
        in_specs=placed,
        out_specs=(
            P("tensor", "dp", None),
            P("tensor", "dp", None),
            P("dp"),
            P("dp"),
            P("dp", None, "tensor"),
            P(None, "tensor", "dp"),
            P("tensor", "dp"),
            P("dp"),
            P("dp"),
            P("dp"),
            P("dp", "tensor"),
            P("tensor", "dp"),
            P("tensor", "dp"),
            P("dp"),
        ),
        check_vma=False,
    )
```

```python
import jax
import jax.numpy as jnp
from jax import lax
from jax.experimental import pallas as pl
from jax.experimental.pallas import tpu as pltpu
from jax.sharding import PartitionSpec as P

HD = 64
EPSILON = 1e-06
NEG_FILL = -1e30
LOW = jnp.bfloat16
FULL = jnp.float32
ORDER = (0, 2, 4, 6, 1, 3, 5, 7)
SMALL_ROWS = 16
VMEM_LIMIT = 60 * 1024 * 1024
ROWS = (((1,), (1,)), ((), ()))
PLAIN = (((1,), (0,)), ((), ()))
DEEP = (((0,), (0,)), ((), ()))


def dot(left, right, contract=PLAIN):
    return lax.dot_general(left, right, contract, preferred_element_type=FULL)


def normalize(rows):
    average = jnp.mean(rows, axis=-1, keepdims=True)
    centered = rows - average
    variance = jnp.mean(centered * centered, axis=-1, keepdims=True)
    scaling = lax.rsqrt(variance + EPSILON)
    return centered * scaling, scaling


def norm_back(grad_output, normal, scaling, gain):
    grad_normal = grad_output * gain
    first_mean = jnp.mean(grad_normal, axis=-1, keepdims=True)
    second_mean = jnp.mean(grad_normal * normal, axis=-1, keepdims=True)
    return scaling * (grad_normal - first_mean - normal * second_mean)


def gelu_parts(v):
    t = 1.0 / (1.0 + 0.23164189 * jnp.abs(v))
    bell = jnp.exp2(v * v * -0.7213475204444817)
    poly = 0.127414796 + t * (
        -0.142248368 + t * (0.7107068705 + t * (-0.7265760135 + t * 0.5307027145))
    )
    tail = poly * (t * bell)
    phi = jnp.where(v < 0.0, tail, 1.0 - tail)
    return v * phi, phi + (v * 0.3989422804014327) * bell


def small_rows(six, pair, row, lanes):
    def wide(values):
        pad = lanes - values.shape[1]
        return jnp.pad(values, ((0, 0), (0, pad))) if pad else values

    first = wide(jnp.concatenate([six[k : k + 1] for k in range(6)], 1))
    at = lax.broadcasted_iota(jnp.int32, (SMALL_ROWS, lanes), 0)
    rows = jnp.where(at == 0, first, jnp.where(at == 1, wide(pair), jnp.where(at == 2, wide(row), 0.0)))
    return rows.astype(LOW)


def call(body, grid, ins, outs, shapes, scratch=(), flops=0, size=0, scalars=None):
    spec = pltpu.PrefetchScalarGridSpec(
        num_scalar_prefetch=0 if scalars is None else 1,
        grid=grid,
        in_specs=[s for _, s in ins],
        out_specs=outs,
        scratch_shapes=list(scratch),
    )
    operands = [a for a, _ in ins]
    if scalars is not None:
        operands = [scalars] + operands
    return pl.pallas_call(
        body,
        grid_spec=spec,
        out_shape=shapes,
        cost_estimate=pl.CostEstimate(flops=flops, bytes_accessed=size, transcendentals=0),
        compiler_params=pltpu.CompilerParams(vmem_limit_bytes=VMEM_LIMIT),
    )(*operands)


def whole(array):
    zeros = (0,) * array.ndim
    return array, pl.BlockSpec(array.shape, lambda *_: zeros, pipeline_mode=pl.Buffered(1))


def fixed(shape):
    zeros = (0,) * len(shape)
    return pl.BlockSpec(shape, lambda *_: zeros)


def out(shape, kind):
    return jax.ShapeDtypeStruct(shape, kind)


class Kernels:
    def __init__(self, blocks, depth, tensor, cut, fan, length, key_length, spots, place):
        self.blocks, self.depth, self.tensor = blocks, depth, tensor
        self.cut, self.fan, self.length, self.key_length = cut, fan, length, key_length
        self.width = blocks * depth
        self.spots = spots
        self.place = place
        self.heads = cut // HD

    def take(self, scalars, ref, o):
        if self.spots is None:
            return ref[:, o * self.depth : (o + 1) * self.depth]
        return ref[:, pl.ds(pl.multiple_of(scalars[o] * self.depth, self.depth), self.depth)]

    def take_all(self, scalars, ref):
        if self.spots is None:
            return ref[...]
        return jnp.concatenate([self.take(scalars, ref, o) for o in range(self.blocks)], 1)

    def put_all(self, scalars, ref, value):
        if self.spots is None:
            ref[...] = value
        else:
            for o in range(self.blocks):
                ref[:, pl.ds(pl.multiple_of(scalars[o] * self.depth, self.depth), self.depth)] = (
                    value[:, o * self.depth : (o + 1) * self.depth]
                )

    def scalars(self):
        spots = jnp.arange(self.blocks, dtype=jnp.int32) if self.spots is None else self.spots
        return jnp.concatenate([spots, self.place[None]])

    def group(self, scalars, t):
        return t ^ scalars[self.blocks]

    def weight_specs(self, arrays, columns, index):
        return [
            (a, pl.BlockSpec((1, a.shape[1], columns), lambda *g, index=index: index(*g)))
            for a in arrays
        ]

    def join(self, refs, left=0, right=None):
        right = refs[0].shape[2] if right is None else right
        return jnp.concatenate([r[0, : self.depth, left:right] for r in refs], 0)

    def pack(self, qkv, proj, reduce, six, pair, row):
        cut, depth, fan = self.cut, self.depth, self.fan

        def body(qkv_ref, proj_ref, reduce_ref, six_ref, pair_ref, row_ref, first_ref, turned_ref):
            for c in range(3):
                first_ref[:depth, c * cut : (c + 1) * cut] = qkv_ref[c]
            first_ref[:depth, 3 * cut :] = proj_ref[...].T
            first_ref[depth:, :] = small_rows(six_ref[...], pair_ref[...], row_ref[...], 4 * cut)
            turned_ref[...] = reduce_ref[...].T

        return call(
            body,
            (1,),
            [whole(a) for a in (qkv, proj, reduce, six, pair, row)],
            [fixed((depth + SMALL_ROWS, 4 * cut)), fixed((depth, fan))],
            [out((depth + SMALL_ROWS, 4 * cut), LOW), out((depth, fan), LOW)],
            size=8 * depth * fan,
        )

    def small_vectors(self, refs):
        depth = self.depth
        rows = [r[0, depth : depth + 8, :].astype(FULL)[0:1] for r in refs]
        return jnp.concatenate(
            [
                jnp.concatenate([row[:, k * depth : (k + 1) * depth] for row in rows], 1)
                for k in range(6)
            ],
            0,
        )

    def small_biases(self, refs):
        cut, depth = self.cut, self.depth
        rows = sum(r[0, depth : depth + 8, :].astype(FULL) for r in refs)
        pair = rows[1:2]
        bias = jnp.concatenate([pair[:, :cut], jnp.zeros((1, cut), FULL), pair[:, cut : 2 * cut]], 1)
        return bias, rows[2:3]

    def project(self, x, weights):
        cut, length, width, fan = self.cut, self.length, self.width, self.fan

        def body(scalars, x_ref, *refs):
            w_refs = refs[: self.blocks]
            normed_ref, proj_ref, vec_ref, row_ref = refs[self.blocks :]

            @pl.when(pl.program_id(0) == 0)
            def _():
                vectors = self.small_vectors(w_refs)
                vec_ref[...] = vectors
                normal, _ = normalize(self.take_all(scalars, x_ref).astype(FULL))
                normed_ref[...] = (normal * vectors[0:1] + vectors[1:2]).astype(LOW)

            bias, row_ref[...] = self.small_biases(w_refs)
            proj = dot(normed_ref[...], self.join(w_refs, 0, 3 * cut)) + bias
            proj_ref[0] = proj.astype(LOW)

        return call(
            body,
            (self.tensor,),
            [whole(x)] + self.weight_specs(weights, 4 * cut, lambda j, *_: (j, 0, 0)),
            [
                fixed((length, width)),
                pl.BlockSpec((1, length, 3 * cut), lambda j, _: (j, 0, 0)),
                fixed((6, width)),
                pl.BlockSpec((1, fan), lambda j, _: (0, j)),
            ],
            [
                out((length, width), LOW),
                out((self.tensor, length, 3 * cut), LOW),
                out((6, width), FULL),
                out((1, fan * self.tensor), FULL),
            ],
            flops=2 * length * width * 3 * cut * self.tensor,
            size=16 * width * width,
            scalars=self.scalars(),
        )

    def attend_heads(self, own_ref, full_ref, mask_ref, att_ref, log_ref):
        cut, length = self.cut, self.length
        valid = mask_ref[...] > 0
        lane = lax.broadcasted_iota(jnp.int32, (length, 128), 1)
        logs = jnp.zeros((length, 128), FULL)
        for h in range(self.heads):
            at = h * HD
            q = own_ref[0, :, at : at + HD] * LOW(HD ** (-0.5))
            k = full_ref[0, :, cut + at : cut + at + HD]
            v = full_ref[0, :, 2 * cut + at : 2 * cut + at + HD]
            scores = jnp.where(valid, dot(q, k, ROWS), NEG_FILL)
            highest = jnp.max(scores, axis=-1, keepdims=True)
            expanded = jnp.exp(scores - highest)
            totals = jnp.sum(expanded, axis=-1, keepdims=True)
            att = dot(expanded.astype(LOW), v) * (1.0 / totals)
            att_ref[:, at : at + HD] = att.astype(LOW)
            logs = jnp.where(lane == h, highest + jnp.log(totals), logs)
        log_ref[0] = logs.T[:8]

    def back_heads(self, own_ref, full_ref, log_ref, mask_ref, grad_att, out_ref, kind, pair_ref=None):
        cut = self.cut
        valid = mask_ref[...] > 0
        for h in range(self.heads):
            at = h * HD
            q = own_ref[0, :, at : at + HD] * LOW(HD ** (-0.5))
            k = full_ref[0, :, cut + at : cut + at + HD]
            v = full_ref[0, :, 2 * cut + at : 2 * cut + at + HD]
            grad = grad_att[:, at : at + HD]
            scores = jnp.where(valid, dot(k, q, ROWS), NEG_FILL)
            probs = jnp.exp(scores - log_ref[0, h : h + 1, :])
            products = probs * dot(v, grad, ROWS)
            inner = jnp.sum(products, axis=0, keepdims=True)
            grad_scores = (products - probs * inner).astype(LOW)
            grad_v = dot(probs.astype(LOW), grad).astype(kind)
            grad_k = dot(grad_scores, q).astype(kind)
            grad_q = (dot(grad_scores, k, DEEP) * HD ** (-0.5)).astype(LOW)
            if pair_ref is None:
                out_ref[:, at : at + HD] = grad_q
                out_ref[:, cut + at : cut + at + HD] = grad_k
                out_ref[:, 2 * cut + at : 2 * cut + at + HD] = grad_v
            else:
                out_ref[0, :, at : at + HD] = grad_q
                pair_ref[0, :, at : at + HD] = grad_k
                pair_ref[0, :, cut + at : cut + at + HD] = grad_v

    def attend(self, own, full, mask_row):
        cut, length, keys = self.cut, self.length, self.key_length

        def body(own_ref, full_ref, mask_ref, att_ref, log_ref):
            self.attend_heads(own_ref, full_ref, mask_ref, att_ref, log_ref)

        return call(
            body,
            (self.tensor,),
            [
                (own, pl.BlockSpec((1, length, 3 * cut), lambda j, *_: (j, 0, 0))),
                (full, pl.BlockSpec((1, keys, 3 * cut), lambda j, *_: (j, 0, 0))),
                whole(mask_row),
            ],
            [
                pl.BlockSpec((length, cut), lambda j: (0, j)),
                pl.BlockSpec((1, 8, length), lambda j, *_: (j, 0, 0)),
            ],
            [out((length, self.width), LOW), out((self.tensor, 8, length), FULL)],
            flops=16 * length * keys * self.width,
            size=16 * length * self.width,
        )

    def close_attention(self, attended, x, vectors, weights):
        cut, length, width = self.cut, self.length, self.width

        def body(scalars, att_ref, x_ref, vec_ref, *refs):
            w_refs = refs[: self.blocks]
            middle_ref, normed_ref = refs[self.blocks :]
            j = pl.program_id(0)

            @pl.when(j == 0)
            def _():
                middle_ref[...] = self.take_all(scalars, x_ref).astype(FULL) + vec_ref[2:3]

            middle_ref[...] += dot(att_ref[...], self.join(w_refs), ROWS)

            @pl.when(j == self.tensor - 1)
            def _():
                normal, _ = normalize(middle_ref[...])
                normed_ref[...] = (normal * vec_ref[3:4] + vec_ref[4:5]).astype(LOW)

        return call(
            body,
            (self.tensor,),
            [
                (attended, pl.BlockSpec((length, cut), lambda j, _: (0, j))),
                whole(x),
                whole(vectors),
            ]
            + self.weight_specs(weights, cut, lambda j, *_: (j, 0, 3)),
            [
                pl.BlockSpec((length, width), lambda j, _: (0, 0)),
                pl.BlockSpec((length, width), lambda j, _: (0, 0)),
            ],
            [out((length, width), FULL), out((length, width), LOW)],
            flops=2 * length * width * width,
            size=12 * length * width,
            scalars=self.scalars(),
        )

    def tile(self):
        return self.fan

    def expand(self, normed, row, weights, own_first):
        length, fan = self.length, self.fan
        total = fan * self.tensor

        def body(scalars, normed_ref, row_ref, *refs):
            w_refs = refs[: self.blocks]
            hidden_ref, slope_ref = refs[self.blocks :]
            before = dot(normed_ref[...], self.join(w_refs)) + row_ref[...]
            hidden, slope = gelu_parts(before)
            hidden_ref[...] = hidden.astype(LOW)
            slope_ref[...] = slope.astype(LOW)

        def row_map(j, s):
            return (0, self.group(s, j) if own_first else j)

        return call(
            body,
            (self.tensor,),
            [whole(normed), (row, pl.BlockSpec((1, fan), row_map))]
            + self.weight_specs(weights, fan, lambda j, *_: (j, 0, 0)),
            [pl.BlockSpec((length, fan), lambda j, _: (0, j))] * 2,
            [out((length, total), LOW)] * 2,
            flops=2 * length * self.width * total,
            size=4 * length * total,
            scalars=self.scalars(),
        )

    def reduce(self, hidden, middle, vectors, weights):
        length, width, tile = self.length, self.width, self.tile()
        per = self.fan // tile
        steps = self.tensor * per

        def body(scalars, hidden_ref, middle_ref, vec_ref, *refs):
            w_refs = refs[: self.blocks]
            out_ref, total = refs[self.blocks :]
            n = pl.program_id(0)

            @pl.when(n == 0)
            def _():
                total[...] = middle_ref[...] + vec_ref[5:6]

            total[...] += dot(hidden_ref[...], self.join(w_refs), ROWS)

            @pl.when(n == steps - 1)
            def _():
                self.put_all(scalars, out_ref, total[...].astype(LOW))

        return call(
            body,
            (steps,),
            [
                (hidden, pl.BlockSpec((length, tile), lambda n, _: (0, n))),
                whole(middle),
                whole(vectors),
            ]
            + self.weight_specs(weights, tile, lambda n, *_: (n // per, 0, n % per)),
            [pl.BlockSpec((length, width), lambda n, _: (0, 0))],
            [out((length, width), LOW)],
            [pltpu.VMEM((length, width), FULL)],
            flops=2 * length * width * self.fan * self.tensor,
            size=2 * length * self.fan * self.tensor,
            scalars=self.scalars(),
        )[0]

    def turn(self, scalars, ref, out_ref, plain=False):
        for o in range(self.blocks):
            at = o * self.depth
            block = self.take(scalars, ref, o) if plain else ref[:, at : at + self.depth]
            out_ref[at : at + self.depth, :] = block.T

    def put_halves(self, kept_ref, sent_ref, j, left, grad):
        count, columns = self.blocks // 2, grad.shape[1]
        rows = count * self.depth
        for ref, part in ((kept_ref, grad[:rows]), (sent_ref, grad[rows:])):
            ref[:, j, : self.depth, left : left + columns] = part.reshape(
                count, self.depth, columns
            )

    def weight_grad(self, left, rights, plain):
        length, depth, count = self.length, self.depth, self.blocks // 2
        pieces = [r.shape[2] if r.ndim == 3 else r.shape[1] // self.tensor for r in rights]
        columns = sum(pieces)

        def body(scalars, left_ref, *refs):
            r_refs = refs[: len(rights)]
            kept_ref, sent_ref, turned = refs[len(rights) :]

            @pl.when(pl.program_id(0) == 0)
            def _():
                self.turn(scalars, left_ref, turned, plain)

            at = 0
            for r, size in zip(r_refs, pieces, strict=True):
                right = r[0] if len(r.shape) == 3 else r[...]
                grad = dot(turned[...], right).astype(LOW)
                self.put_halves(kept_ref, sent_ref, 0, at, grad)
                at += size

        ins = [whole(left)]
        for r, size in zip(rights, pieces, strict=True):
            if r.ndim == 3:
                ins.append((r, pl.BlockSpec((1, length, size), lambda j, _: (j, 0, 0))))
            else:
                ins.append((r, pl.BlockSpec((length, size), lambda j, _: (0, j))))
        return call(
            body,
            (self.tensor,),
            ins,
            [pl.BlockSpec((count, 1, depth, columns), lambda j, _: (0, j, 0, 0))] * 2,
            [out((count, self.tensor, depth, columns), LOW)] * 2,
            [pltpu.VMEM((self.width, length), LOW)],
            flops=2 * length * self.width * columns * self.tensor,
            size=2 * self.width * columns * self.tensor,
            scalars=self.scalars(),
        )

    def feed_back(self, cotangent, slope, normed, middle, vectors, reduces, expands):
        length, width, fan, depth = self.length, self.width, self.fan, self.depth
        count = self.blocks // 2

        def body(scalars, cot_ref, slope_ref, normed_ref, middle_ref, vec_ref, *refs):
            r_refs, e_refs = refs[: self.blocks], refs[self.blocks : 2 * self.blocks]
            (full_ref, low_ref, sum_ref, row_ref, kept_ref, sent_ref, cot, turned, total) = refs[
                2 * self.blocks :
            ]
            j = pl.program_id(0)

            @pl.when(j == 0)
            def _():
                cot[...] = self.take_all(scalars, cot_ref)
                self.turn(scalars, normed_ref, turned)
                total[...] = jnp.zeros_like(total)

            grad = dot(cot[...], self.join(r_refs)) * slope_ref[...].astype(FULL)
            grad = grad.astype(LOW)
            row_ref[...] = jnp.sum(grad.astype(FULL), axis=0, keepdims=True)
            self.put_halves(kept_ref, sent_ref, 0, 0, dot(turned[...], grad).astype(LOW))
            total[...] += dot(grad, self.join(e_refs), ROWS)

            @pl.when(j == self.tensor - 1)
            def _():
                grad = total[...]
                normal, scaling = normalize(middle_ref[...])
                grad_output = cot[...].astype(FULL)
                result = grad_output + norm_back(grad, normal, scaling, vec_ref[3:4])
                full_ref[...] = result
                low_ref[...] = result.astype(LOW)
                sum_ref[0:1] = jnp.sum(result, axis=0, keepdims=True)
                sum_ref[1:2] = jnp.sum(grad * normal, axis=0, keepdims=True)
                sum_ref[2:3] = jnp.sum(grad, axis=0, keepdims=True)
                sum_ref[3:4] = jnp.sum(grad_output, axis=0, keepdims=True)

        return call(
            body,
            (self.tensor,),
            [
                whole(cotangent),
                (slope, pl.BlockSpec((length, fan), lambda j, _: (0, j))),
                whole(normed),
                whole(middle),
                whole(vectors),
            ]
            + self.weight_specs(reduces, fan, lambda j, *_: (j, 0, 0))
            + self.weight_specs(expands, fan, lambda j, *_: (j, 0, 0)),
            [
                fixed((length, width)),
                fixed((length, width)),
                fixed((4, width)),
                pl.BlockSpec((1, fan), lambda j, _: (0, j)),
            ]
            + [pl.BlockSpec((count, 1, depth, fan), lambda j, _: (0, j, 0, 0))] * 2,
            [
                out((length, width), FULL),
                out((length, width), LOW),
                out((4, width), FULL),
                out((1, fan * self.tensor), FULL),
            ]
            + [out((count, self.tensor, depth, fan), LOW)] * 2,
            [
                pltpu.VMEM((length, width), LOW),
                pltpu.VMEM((width, length), LOW),
                pltpu.VMEM((length, width), FULL),
            ],
            flops=6 * length * width * fan * self.tensor,
            size=16 * width * fan,
            scalars=self.scalars(),
        )

    def attend_back(self, own, full, logs, mask_column, grad_branch, weights, kind):
        cut, length, keys = self.cut, self.length, self.key_length

        def body(own_ref, full_ref, log_ref, mask_ref, branch_ref, *refs):
            w_refs = refs[: self.blocks]
            query_ref, pair_ref = refs[self.blocks :]
            grad_att = dot(branch_ref[...], self.join(w_refs)).astype(LOW)
            self.back_heads(
                own_ref, full_ref, log_ref, mask_ref, grad_att, query_ref, kind, pair_ref
            )

        return call(
            body,
            (self.tensor,),
            [
                (own, pl.BlockSpec((1, length, 3 * cut), lambda j, *_: (j, 0, 0))),
                (full, pl.BlockSpec((1, keys, 3 * cut), lambda j, *_: (j, 0, 0))),
                (logs, pl.BlockSpec((1, 8, length), lambda j, *_: (j, 0, 0))),
                whole(mask_column),
                whole(grad_branch),
            ]
            + self.weight_specs(weights, cut, lambda j, *_: (j, 0, 3)),
            [
                pl.BlockSpec((1, length, cut), lambda j, *_: (j, 0, 0)),
                pl.BlockSpec((1, keys, 2 * cut), lambda j, *_: (j, 0, 0)),
            ],
            [
                out((self.tensor, length, cut), LOW),
                out((self.tensor, keys, 2 * cut), kind),
            ],
            flops=40 * length * keys * self.width,
            size=20 * length * self.width,
        )

    def project_back(self, grad_query, grad_pair, x, grad_middle, vectors, weights):
        cut, length, width = self.cut, self.length, self.width

        def body(scalars, query_ref, pair_ref, x_ref, grad_ref, vec_ref, *refs):
            w_refs = refs[: self.blocks]
            out_ref, sum_ref, pair_sum_ref, total = refs[self.blocks :]
            j = pl.program_id(0)

            @pl.when(j == 0)
            def _():
                total[...] = jnp.zeros_like(total)

            query, pair = query_ref[0], pair_ref[0]
            total[...] += dot(query, self.join(w_refs, 0, cut), ROWS) + dot(
                pair, self.join(w_refs, cut, 3 * cut), ROWS
            )
            pair_sum_ref[0, :, :cut] = jnp.sum(query.astype(FULL), axis=0, keepdims=True)
            pair_sum_ref[0, :, cut:] = jnp.sum(pair.astype(FULL), axis=0, keepdims=True)

            @pl.when(j == self.tensor - 1)
            def _():
                grad = total[...]
                normal, scaling = normalize(self.take_all(scalars, x_ref).astype(FULL))
                result = grad_ref[...] + norm_back(grad, normal, scaling, vec_ref[0:1])
                self.put_all(scalars, out_ref, result.astype(LOW))
                sum_ref[0:1] = jnp.sum(grad * normal, axis=0, keepdims=True)
                sum_ref[1:2] = jnp.sum(grad, axis=0, keepdims=True)

        return call(
            body,
            (self.tensor,),
            [
                (grad_query, pl.BlockSpec((1, length, cut), lambda j, _: (j, 0, 0))),
                (grad_pair, pl.BlockSpec((1, length, 2 * cut), lambda j, _: (j, 0, 0))),
                whole(x),
                whole(grad_middle),
                whole(vectors),
            ]
            + self.weight_specs(weights, 4 * cut, lambda j, *_: (j, 0, 0)),
            [
                pl.BlockSpec((length, width), lambda j, _: (0, 0)),
                pl.BlockSpec((2, width), lambda j, _: (0, 0)),
                pl.BlockSpec((1, 1, 3 * cut), lambda j, _: (j, 0, 0)),
            ],
            [out((length, width), LOW), out((2, width), FULL), out((self.tensor, 1, 3 * cut), FULL)],
            [pltpu.VMEM((length, width), FULL)],
            flops=2 * length * width * 3 * cut * self.tensor,
            size=8 * length * width,
            scalars=self.scalars(),
        )

    def attention(self, x, mask_row, weights, start, count, before=None):
        cut, length, width, fan = self.cut, self.length, self.width, self.fan
        first, final = before is None, before is not None

        def body(scalars, x_ref, mask_ref, *refs):
            w_refs, refs = refs[: self.blocks], refs[self.blocks :]
            if first:
                own_ref, att_ref, log_ref, row_ref, middle_ref, normed_ref, vec_ref = refs[:7]
                refs = refs[7:]
            else:
                middle_in, normed_ref, vec_ref = refs[:3]
                own_ref, att_ref, log_ref, row_ref, middle_ref = refs[3:8]
                refs = refs[8:]
            j = pl.program_id(0)

            @pl.when(j == 0)
            def _():
                if first:
                    vectors = self.small_vectors(w_refs)
                    vec_ref[...] = vectors
                    rows = self.take_all(scalars, x_ref).astype(FULL)
                    middle_ref[...] = rows + vectors[2:3]
                    normal, _ = normalize(rows)
                    normed_ref[...] = (normal * vectors[0:1] + vectors[1:2]).astype(LOW)
                else:
                    middle_ref[...] = middle_in[...]

            bias, row_ref[...] = self.small_biases(w_refs)
            own = dot(normed_ref[...], self.join(w_refs, 0, 3 * cut)) + bias
            own_ref[0] = own.astype(LOW)
            self.attend_heads(own_ref, own_ref, mask_ref, att_ref, log_ref)
            middle_ref[...] += dot(att_ref[...], self.join(w_refs, 3 * cut, 4 * cut), ROWS)

            if final:
                (two_ref,) = refs

                @pl.when(j == count - 1)
                def _():
                    normal, _ = normalize(middle_ref[...])
                    two_ref[...] = (normal * vec_ref[3:4] + vec_ref[4:5]).astype(LOW)

        outs = [
            (pl.BlockSpec((1, length, 3 * cut), lambda j, _: (j, 0, 0)), out((count, length, 3 * cut), LOW)),
            (pl.BlockSpec((length, cut), lambda j, _: (0, j)), out((length, count * cut), LOW)),
            (pl.BlockSpec((1, 8, length), lambda j, _: (j, 0, 0)), out((count, 8, length), FULL)),
            (pl.BlockSpec((1, fan), lambda j, _: (0, j)), out((1, count * fan), FULL)),
            (fixed((length, width)), out((length, width), FULL)),
        ]
        if first:
            outs.append((fixed((length, width)), out((length, width), LOW)))
            outs.append((fixed((6, width)), out((6, width), FULL)))
        if final:
            outs.append((fixed((length, width)), out((length, width), LOW)))
        return call(
            body,
            (count,),
            [whole(x), whole(mask_row)]
            + self.weight_specs(weights, 4 * cut, lambda j, s: (self.group(s, start + j), 0, 0))
            + [whole(a) for a in before or ()],
            [spec for spec, _ in outs],
            [shape for _, shape in outs],
            flops=(8 * length * width * width + 4 * length * length * width) * count // self.tensor,
            size=16 * width * width,
            scalars=self.scalars(),
        )

    def attention_back(
        self, own, logs, mask_column, branch, attended, normed, weights, start, count, before=None, closing=None
    ):
        cut, length, width, depth = self.cut, self.length, self.width, self.depth
        half, lanes = self.blocks // 2, 4 * self.cut
        first, final = before is None, closing is not None
        rows = depth + SMALL_ROWS * self.tensor // count if final else depth

        def body(scalars, own_ref, log_ref, mask_ref, branch_ref, att_ref, normed_ref, *refs):
            w_refs, refs = refs[: self.blocks], refs[self.blocks :]
            if not first:
                total_in, pairs_in = refs[:2]
                refs = refs[2:]
            if final:
                x_ref, grad_ref, sums_ref, row_ref, vec_ref = refs[:5]
                refs = refs[5:]
            kept_ref, sent_ref, out_ref = refs[:3]
            refs = refs[3:]
            if final:
                total, pairs_ref, turned, turned_two, part = refs
            else:
                pairs_ref, turned, turned_two, part = refs
                total = out_ref
            j = pl.program_id(0)

            @pl.when(j == 0)
            def _():
                self.turn(scalars, normed_ref, turned)
                self.turn(scalars, branch_ref, turned_two)
                total[...] = jnp.zeros((length, width), FULL) if first else total_in[...]
                if not first:
                    pairs_ref[count:, :] = pairs_in[...]

            grad_att = dot(branch_ref[...], self.join(w_refs, 3 * cut, lanes)).astype(LOW)
            self.back_heads(own_ref, own_ref, log_ref, mask_ref, grad_att, part, LOW)
            grad = part[...]
            total[...] += dot(grad, self.join(w_refs, 0, 3 * cut), ROWS)
            pairs_ref[pl.ds(j, 1), :] = jnp.sum(grad.astype(FULL), axis=0, keepdims=True)
            self.put_halves(kept_ref, sent_ref, j, 0, dot(turned[...], grad).astype(LOW))
            self.put_halves(
                kept_ref, sent_ref, j, 3 * cut, dot(turned_two[...], att_ref[...]).astype(LOW)
            )

            if final:

                @pl.when(j == count - 1)
                def _():
                    grad = total[...]
                    normal, scaling = normalize(self.take_all(scalars, x_ref).astype(FULL))
                    result = grad_ref[...] + norm_back(grad, normal, scaling, vec_ref[0:1])
                    self.put_all(scalars, out_ref, result.astype(LOW))
                    gain = jnp.sum(grad * normal, axis=0, keepdims=True)
                    shift = jnp.sum(grad, axis=0, keepdims=True)
                    six = jnp.concatenate([gain, shift, sums_ref[...]], 0)
                    for t in range(self.tensor):
                        pair = jnp.concatenate(
                            [pairs_ref[t : t + 1, :cut], pairs_ref[t : t + 1, 2 * cut :]], 1
                        )
                        at = self.group(scalars, t) * self.fan
                        row = row_ref[:, pl.ds(pl.multiple_of(at, self.fan), self.fan)]
                        at = depth + SMALL_ROWS * (t // count)
                        for o in range(self.blocks):
                            ref = (kept_ref, sent_ref)[o // half]
                            ref[o % half, t % count, at : at + SMALL_ROWS, :] = small_rows(
                                six[:, o * depth : (o + 1) * depth], pair, row, lanes
                            )

        ins = [
            (own, pl.BlockSpec((1, length, 3 * cut), lambda j, _: (j, 0, 0))),
            (logs, pl.BlockSpec((1, 8, length), lambda j, _: (j, 0, 0))),
            whole(mask_column),
            whole(branch),
            (attended, pl.BlockSpec((length, cut), lambda j, _: (0, j))),
            whole(normed),
        ]
        ins += self.weight_specs(weights, lanes, lambda j, s: (self.group(s, start + j), 0, 0))
        ins += [whole(a) for a in (before or ()) + (closing or ())]
        pair_rows = self.tensor if final else count
        outs = [(fixed((half, count, rows, lanes)), out((half, count, rows, lanes), LOW))] * 2
        outs.append((fixed((length, width)), out((length, width), LOW if final else FULL)))
        scratch = [
            pltpu.VMEM((width, length), LOW),
            pltpu.VMEM((width, length), LOW),
            pltpu.VMEM((length, 3 * cut), LOW),
        ]
        if final:
            scratch = [pltpu.VMEM((length, width), FULL), pltpu.VMEM((pair_rows, 3 * cut), FULL)] + scratch
        else:
            outs.append((fixed((pair_rows, 3 * cut)), out((pair_rows, 3 * cut), FULL)))
        return call(
            body,
            (count,),
            ins,
            [spec for spec, _ in outs],
            [shape for _, shape in outs],
            scratch,
            flops=(16 * length * width * width + 10 * length * length * width) * count // self.tensor,
            size=32 * width * width,
            scalars=self.scalars(),
        )


class Layout:
    def __init__(self, sizes, images):
        self.dp, self.tensor = sizes["dp"], sizes["tensor"]
        self.images = images
        self.groups = self.tensor // images
        self.near = self.dp == 8
        self.me = lax.axis_index("dp")
        self.place = lax.axis_index("tensor")

    def swap(self, array, bit):
        return lax.ppermute(array, "dp", [(k, k ^ bit) for k in range(self.dp)])

    def swap_tensor(self, array, step):
        return lax.ppermute(array, "tensor", [(k, k ^ step) for k in range(self.tensor)])

    def spots(self):
        if not self.near:
            return None
        return jnp.array(ORDER, jnp.int32) ^ self.me.astype(jnp.int32)

    def ordered(self, array):
        if not self.near:
            return array
        return jnp.concatenate(
            [lax.dynamic_slice_in_dim(array, self.me ^ r, 1, 0) for r in ORDER], 0
        )

    def plain(self, array):
        if not self.near:
            return array
        pieces = []
        for block in range(8):
            r = self.me ^ block
            pieces.append(lax.dynamic_slice_in_dim(array, (r & 1) * 4 + (r >> 1), 1, 0))
        return jnp.concatenate(pieces, 0)

    def gather(self, shard, beside=None):
        line = lax.all_gather(shard, "tensor", axis=0)
        if beside is not None:
            line, beside[:] = lax.optimization_barrier((line, beside))
        if not self.near:
            return list(lax.all_gather(line, "dp", axis=0))
        half = self.tensor // 2
        by_x = self.swap(line, 2)
        by_y = self.swap(line, 4)
        top = self.swap(by_y[:half], 2)
        bottom = self.swap(by_x[half:], 4)
        far = jnp.concatenate([top, bottom], 0)
        mine = [line, by_x, by_y, far]
        return mine + [self.swap(block, 1) for block in mine]

    def scatter(self, kept, sent):
        if not self.near:
            return lax.psum_scatter(jnp.concatenate([kept, sent], 0), "dp", scatter_dimension=0)
        came = self.swap(sent, 1)
        half = kept.shape[1] // 2

        def add(*parts):
            return sum(part.astype(FULL) for part in parts).astype(LOW)

        top = self.swap(add(kept[3, :half], came[3, :half]), 2)
        bottom = self.swap(add(kept[3, half:], came[3, half:]), 4)
        x_block = jnp.concatenate(
            [add(kept[1, :half], came[1, :half]), add(kept[1, half:], came[1, half:], bottom)],
            0,
        )
        y_block = jnp.concatenate(
            [add(kept[2, :half], came[2, :half], top), add(kept[2, half:], came[2, half:])],
            0,
        )
        by_x = self.swap(x_block, 2)
        by_y = self.swap(y_block, 4)
        return add(kept[0], came[0], by_x, by_y)

    def scatter_line(self, total):
        total = lax.psum_scatter(total, "tensor", scatter_dimension=0)
        return total.astype(FULL)

    def scatter_near(self, near, far, lower):
        count = near.shape[0]
        total = near[0, :lower].astype(FULL)
        for step in range(1, count):
            total += self.swap_tensor(near[step, :lower], step).astype(FULL)
        for step in range(count, self.tensor):
            body = self.swap_tensor(far[step - count], step).astype(FULL)
            below = self.swap_tensor(near[step - count, lower:], step).astype(FULL)
            total += jnp.concatenate([body, below], 0)
        return total

    def split(self, array):
        spot = self.place % self.images
        return [
            lax.dynamic_index_in_dim(array, spot ^ step, 1, keepdims=False)
            for step in range(self.images)
        ]

    def to_image(self, blocks):
        came = [
            self.swap_tensor(block, step)
            for step, block in enumerate(blocks)
            if step
        ]
        return jnp.concatenate(blocks[:1] + came, 0)

    def from_image(self, array):
        spot = self.place % self.images
        rows = array.shape[0] // self.images
        blocks = [array[:rows]]
        for step in range(1, self.images):
            part = array[step * rows : (step + 1) * rows]
            blocks.append(self.swap_tensor(part, step))
        return jnp.stack(
            [self.pick(blocks, spot ^ image) for image in range(self.images)], 1
        )

    def pick(self, blocks, index):
        chosen = blocks[0]
        for k in range(1, len(blocks)):
            chosen = jnp.where(index == k, blocks[k], chosen)
        return chosen

    def halves(self, array):
        parts = [array]
        for group in range(1, self.groups):
            parts.append(self.swap_tensor(array, group * self.images))
        return parts[0] if len(parts) == 1 else jnp.concatenate(parts, 1)

    def halves_back(self, array):
        rows = array.shape[1] // self.groups
        total = array[:, :rows]
        for group in range(1, self.groups):
            total = total + self.swap_tensor(array[:, group * rows : (group + 1) * rows], group * self.images)
        return total.astype(LOW)

    def valid_keys(self, key_mask):
        rows = key_mask.shape[1] // self.tensor
        mine = lax.dynamic_index_in_dim(
            key_mask, self.place % self.images, 0, keepdims=False
        )
        return jnp.concatenate(
            [
                lax.dynamic_slice_in_dim(mine, (self.place ^ block) * rows, rows, 0)
                for block in range(self.tensor)
            ]
        )


def shards(
    sizes,
    tokens,
    attn_gain,
    attn_shift,
    qkv_weight,
    query_value_bias,
    proj_weight,
    proj_bias,
    mlp_gain,
    mlp_shift,
    expand_weight,
    expand_bias,
    reduce_weight,
    reduce_bias,
    key_mask,
    cotangent,
):
    lay = Layout(sizes, tokens.shape[1])
    depth = attn_gain.shape[0]
    cut = qkv_weight.shape[2]
    fan = expand_weight.shape[1]
    heads = cut // HD
    slots = query_value_bias.shape[2]
    length = tokens.shape[0] * lay.images
    keys = length * lay.groups
    do = Kernels(lay.dp, depth, lay.tensor, cut, fan, length, keys, lay.spots(), lay.place.astype(jnp.int32))

    token_blocks, cot_blocks = lay.split(tokens), lay.split(cotangent)
    lanes, count = 4 * cut, expand_bias.size
    six = jnp.stack([attn_gain, attn_shift, proj_bias, mlp_gain, mlp_shift, reduce_bias]).astype(FULL)
    owner = jnp.arange(lay.dp)[:, None] == lay.me
    pair = jnp.where(owner, query_value_bias.astype(FULL)[:, :, None], 0.0).reshape(1, -1)
    row = jnp.where(owner, expand_bias.astype(FULL), 0.0).reshape(1, -1)
    first, turned = do.pack(qkv_weight.transpose(1, 0, 2), proj_weight, reduce_weight, six, pair, row)
    beside = token_blocks + cot_blocks
    first_blocks = lay.gather(first, beside)
    token_blocks, cot_blocks = beside[: lay.images], beside[lay.images :]
    image = lay.to_image(token_blocks)
    expand_blocks = lay.gather(expand_weight)
    reduce_blocks = lay.gather(turned)
    cot_image = lay.to_image(cot_blocks)
    mask = lay.valid_keys(key_mask)

    together = lay.groups == 1
    if together:
        split = lay.tensor // 2
        own_two, attended_two, logs_two, row_two, middle, normed_one, vectors = do.attention(
            image, mask[None], first_blocks, split, split
        )
        own, attended, logs, row, middle, normed_two = do.attention(
            image, mask[None], first_blocks, 0, split, (middle, normed_one, vectors)
        )
        expand_row = jnp.concatenate([row, row_two], 1)
    else:
        normed_one, own, vectors, expand_row = do.project(image, first_blocks)
        full = lay.halves(own)
        attended, logs = do.attend(own, full, mask[None])
        middle, normed_two = do.close_attention(attended, image, vectors, first_blocks)
    hidden, slope = do.expand(normed_two, expand_row, expand_blocks, together)
    block_output = lay.from_image(do.reduce(hidden, middle, vectors, reduce_blocks))

    halves = do.weight_grad(cot_image, [hidden], True)
    reduce_grad = lay.scatter_line(lay.scatter(*halves)).T
    grad_middle, grad_branch, sums, row_grad, *halves = do.feed_back(
        cot_image, slope, normed_two, middle, vectors, reduce_blocks, expand_blocks
    )
    expand_grad = lay.scatter_line(lay.scatter(*halves))
    if together:
        column = mask[:, None]
        *halves, total, pairs = do.attention_back(
            own_two, logs_two, column, grad_branch, attended_two, normed_one, first_blocks, split, split
        )
        far = lay.scatter(*halves)
        *halves, tokens_grad = do.attention_back(
            own,
            logs,
            column,
            grad_branch,
            attended,
            normed_one,
            first_blocks,
            0,
            split,
            (total, pairs),
            (image, grad_middle, sums, row_grad, vectors),
        )
        near = lay.scatter(*halves)
        last = lay.scatter_near(near, far, depth + SMALL_ROWS)
    else:
        grad_query, grad_pair = do.attend_back(
            own, full, logs, mask[:, None], grad_branch, first_blocks, FULL
        )
        grad_pair = lay.halves_back(grad_pair)
        tokens_grad, sums_one, pair_sums = do.project_back(
            grad_query, grad_pair, image, grad_middle, vectors, first_blocks
        )
        qkv_halves = do.weight_grad(normed_one, [grad_query, grad_pair], False)
        proj_halves = do.weight_grad(grad_branch, [attended], False)
        six = jnp.concatenate([sums_one, sums], 0)
        pair_rows = jnp.concatenate([pair_sums[:, 0, :cut], pair_sums[:, 0, 2 * cut :]], 1)
        rows = jnp.stack(
            [
                jnp.stack(
                    [
                        small_rows(
                            six[:, o * depth : (o + 1) * depth],
                            pair_rows[t : t + 1],
                            row_grad[:, t * fan : (t + 1) * fan],
                            lanes,
                        )
                        for t in range(lay.tensor)
                    ]
                )
                for o in range(lay.dp)
            ]
        )
        half = lay.dp // 2
        halves = [
            jnp.concatenate([jnp.concatenate([qkv, proj], 3), small], 2)
            for qkv, proj, small in zip(qkv_halves, proj_halves, (rows[:half], rows[half:]), strict=True)
        ]
        last = lay.scatter_line(lay.scatter(*halves))
    tokens_grad = lay.from_image(tokens_grad)
    vector_grads = last[depth, : 6 * depth].reshape(6, depth)
    pair_grad = last[depth + 1, : 2 * cut].reshape(2, heads, HD)
    pair_grad = lax.dynamic_slice_in_dim(pair_grad, lay.me * slots, slots, 2)
    row_part = lax.dynamic_slice_in_dim(last[depth + 2], lay.me * count, count, 0)
    return (
        block_output,
        tokens_grad,
        vector_grads[0],
        vector_grads[1],
        last[:depth, : 3 * cut].reshape(depth, 3, cut),
        pair_grad,
        last[:depth, 3 * cut :].T,
        vector_grads[2],
        vector_grads[3],
        vector_grads[4],
        expand_grad,
        row_part.reshape(expand_bias.shape),
        reduce_grad,
        vector_grads[5],
    )


def solution(mesh):
    placed = (
        P("tensor", "dp", None),
        P("dp"),
        P("dp"),
        P("dp", None, "tensor"),
        P(None, "tensor", "dp"),
        P("tensor", "dp"),
        P("dp"),
        P("dp"),
        P("dp"),
        P("dp", "tensor"),
        P("tensor", "dp"),
        P("tensor", "dp"),
        P("dp"),
        P("dp", None),
        P("tensor", "dp", None),
    )

    def step(*arrays):
        return shards(dict(mesh.shape), *arrays)

    return jax.shard_map(
        step,
        mesh=mesh,
        in_specs=placed,
        out_specs=(
            P("tensor", "dp", None),
            P("tensor", "dp", None),
            P("dp"),
            P("dp"),
            P("dp", None, "tensor"),
            P(None, "tensor", "dp"),
            P("tensor", "dp"),
            P("dp"),
            P("dp"),
            P("dp"),
            P("dp", "tensor"),
            P("tensor", "dp"),
            P("tensor", "dp"),
            P("dp"),
        ),
        check_vma=False,
    )
```

```python
import jax
import jax.numpy as jnp
from jax import lax
from jax.experimental import pallas as pl
from jax.experimental.pallas import tpu as pltpu
from jax.sharding import PartitionSpec as P

HD = 64
EPSILON = 1e-06
NEG_FILL = -1e30
LOW = jnp.bfloat16
FULL = jnp.float32
ORDER = (0, 2, 4, 6, 1, 3, 5, 7)
SMALL_ROWS = 16
MIB = 1024 * 1024
ROWS = (((1,), (1,)), ((), ()))
PLAIN = (((1,), (0,)), ((), ()))
DEEP = (((0,), (0,)), ((), ()))


def dot(left, right, contract=PLAIN):
    return lax.dot_general(left, right, contract, preferred_element_type=FULL)


def normalize(rows):
    average = jnp.mean(rows, axis=-1, keepdims=True)
    centered = rows - average
    variance = jnp.mean(centered * centered, axis=-1, keepdims=True)
    scaling = lax.rsqrt(variance + EPSILON)
    return centered * scaling, scaling


def norm_back(grad_output, normal, scaling, gain):
    grad_normal = grad_output * gain
    first_mean = jnp.mean(grad_normal, axis=-1, keepdims=True)
    second_mean = jnp.mean(grad_normal * normal, axis=-1, keepdims=True)
    return scaling * (grad_normal - first_mean - normal * second_mean)


def gelu_parts(v):
    t = 1.0 / (1.0 + 0.23164189 * jnp.abs(v))
    bell = jnp.exp2(v * v * -0.7213475204444817)
    poly = 0.127414796 + t * (
        -0.142248368 + t * (0.7107068705 + t * (-0.7265760135 + t * 0.5307027145))
    )
    tail = poly * (t * bell)
    phi = jnp.where(v < 0.0, tail, 1.0 - tail)
    return v * phi, phi + (v * 0.3989422804014327) * bell


def small_rows(six, pair, row, lanes):
    def wide(values):
        pad = lanes - values.shape[1]
        return jnp.pad(values, ((0, 0), (0, pad))) if pad else values

    first = wide(jnp.concatenate([six[k : k + 1] for k in range(6)], 1))
    at = lax.broadcasted_iota(jnp.int32, (SMALL_ROWS, lanes), 0)
    rows = jnp.where(at == 0, first, jnp.where(at == 1, wide(pair), jnp.where(at == 2, wide(row), 0.0)))
    return rows.astype(LOW)


def call(body, grid, ins, outs, shapes, scratch=(), flops=0, size=0, scalars=None, room=12):
    spec = pltpu.PrefetchScalarGridSpec(
        num_scalar_prefetch=0 if scalars is None else 1,
        grid=grid,
        in_specs=[s for _, s in ins],
        out_specs=outs,
        scratch_shapes=list(scratch),
    )
    operands = [a for a, _ in ins]
    if scalars is not None:
        operands = [scalars] + operands
    return pl.pallas_call(
        body,
        grid_spec=spec,
        out_shape=shapes,
        cost_estimate=pl.CostEstimate(flops=flops, bytes_accessed=size, transcendentals=0),
        compiler_params=pltpu.CompilerParams(vmem_limit_bytes=room * MIB),
    )(*operands)


def whole(array):
    zeros = (0,) * array.ndim
    return array, pl.BlockSpec(array.shape, lambda *_: zeros, pipeline_mode=pl.Buffered(1))


def fixed(shape):
    zeros = (0,) * len(shape)
    return pl.BlockSpec(shape, lambda *_: zeros)


def out(shape, kind):
    return jax.ShapeDtypeStruct(shape, kind)


class Kernels:
    def __init__(self, blocks, depth, tensor, cut, fan, length, key_length, spots, place):
        self.blocks, self.depth, self.tensor = blocks, depth, tensor
        self.cut, self.fan, self.length, self.key_length = cut, fan, length, key_length
        self.width = blocks * depth
        self.spots = spots
        self.place = place
        self.heads = cut // HD

    def take(self, scalars, ref, o):
        if self.spots is None:
            return ref[:, o * self.depth : (o + 1) * self.depth]
        return ref[:, pl.ds(pl.multiple_of(scalars[o] * self.depth, self.depth), self.depth)]

    def take_all(self, scalars, ref):
        if self.spots is None:
            return ref[...]
        return jnp.concatenate([self.take(scalars, ref, o) for o in range(self.blocks)], 1)

    def put_all(self, scalars, ref, value):
        if self.spots is None:
            ref[...] = value
        else:
            for o in range(self.blocks):
                ref[:, pl.ds(pl.multiple_of(scalars[o] * self.depth, self.depth), self.depth)] = (
                    value[:, o * self.depth : (o + 1) * self.depth]
                )

    def scalars(self):
        spots = jnp.arange(self.blocks, dtype=jnp.int32) if self.spots is None else self.spots
        return jnp.concatenate([spots, self.place[None]])

    def group(self, scalars, t):
        return t ^ scalars[self.blocks]

    def weight_specs(self, arrays, columns, index):
        return [
            (
                pltpu.with_memory_space_constraint(a, pltpu.HBM),
                pl.BlockSpec((1, a.shape[1], columns), lambda *g, index=index: index(*g)),
            )
            for a in arrays
        ]

    def join(self, refs, left=0, right=None):
        right = refs[0].shape[2] if right is None else right
        return jnp.concatenate([r[0, : self.depth, left:right] for r in refs], 0)

    def pack(self, qkv, proj, reduce, six, pair, row):
        cut, depth, fan = self.cut, self.depth, self.fan

        def body(qkv_ref, proj_ref, reduce_ref, six_ref, pair_ref, row_ref, first_ref, turned_ref):
            for c in range(3):
                first_ref[:depth, c * cut : (c + 1) * cut] = qkv_ref[c]
            first_ref[:depth, 3 * cut :] = proj_ref[...].T
            first_ref[depth:, :] = small_rows(six_ref[...], pair_ref[...], row_ref[...], 4 * cut)
            turned_ref[...] = reduce_ref[...].T

        return call(
            body,
            (1,),
            [whole(a) for a in (qkv, proj, reduce, six, pair, row)],
            [fixed((depth + SMALL_ROWS, 4 * cut)), fixed((depth, fan))],
            [out((depth + SMALL_ROWS, 4 * cut), LOW), out((depth, fan), LOW)],
            size=8 * depth * fan,
            room=4,
        )

    def small_vectors(self, refs):
        depth = self.depth
        rows = [r[0, depth : depth + 8, :].astype(FULL)[0:1] for r in refs]
        return jnp.concatenate(
            [
                jnp.concatenate([row[:, k * depth : (k + 1) * depth] for row in rows], 1)
                for k in range(6)
            ],
            0,
        )

    def small_biases(self, refs):
        cut, depth = self.cut, self.depth
        rows = sum(r[0, depth : depth + 8, :].astype(FULL) for r in refs)
        pair = rows[1:2]
        bias = jnp.concatenate([pair[:, :cut], jnp.zeros((1, cut), FULL), pair[:, cut : 2 * cut]], 1)
        return bias, rows[2:3]

    def project(self, x, weights):
        cut, length, width, fan = self.cut, self.length, self.width, self.fan

        def body(scalars, x_ref, *refs):
            w_refs = refs[: self.blocks]
            normed_ref, proj_ref, vec_ref, row_ref = refs[self.blocks :]

            @pl.when(pl.program_id(0) == 0)
            def _():
                vectors = self.small_vectors(w_refs)
                vec_ref[...] = vectors
                normal, _ = normalize(self.take_all(scalars, x_ref).astype(FULL))
                normed_ref[...] = (normal * vectors[0:1] + vectors[1:2]).astype(LOW)

            bias, row_ref[...] = self.small_biases(w_refs)
            proj = dot(normed_ref[...], self.join(w_refs, 0, 3 * cut)) + bias
            proj_ref[0] = proj.astype(LOW)

        return call(
            body,
            (self.tensor,),
            [whole(x)] + self.weight_specs(weights, 4 * cut, lambda j, *_: (j, 0, 0)),
            [
                fixed((length, width)),
                pl.BlockSpec((1, length, 3 * cut), lambda j, _: (j, 0, 0)),
                fixed((6, width)),
                pl.BlockSpec((1, fan), lambda j, _: (0, j)),
            ],
            [
                out((length, width), LOW),
                out((self.tensor, length, 3 * cut), LOW),
                out((6, width), FULL),
                out((1, fan * self.tensor), FULL),
            ],
            flops=2 * length * width * 3 * cut * self.tensor,
            size=16 * width * width,
            scalars=self.scalars(),
        )

    def attend_heads(self, own_ref, full_ref, mask_ref, att_ref, log_ref):
        cut, length = self.cut, self.length
        valid = mask_ref[...] > 0
        lane = lax.broadcasted_iota(jnp.int32, (length, 128), 1)
        logs = jnp.zeros((length, 128), FULL)
        for h in range(self.heads):
            at = h * HD
            q = own_ref[0, :, at : at + HD] * LOW(HD ** (-0.5))
            k = full_ref[0, :, cut + at : cut + at + HD]
            v = full_ref[0, :, 2 * cut + at : 2 * cut + at + HD]
            scores = jnp.where(valid, dot(q, k, ROWS), NEG_FILL)
            highest = jnp.max(scores, axis=-1, keepdims=True)
            expanded = jnp.exp(scores - highest)
            totals = jnp.sum(expanded, axis=-1, keepdims=True)
            att = dot(expanded.astype(LOW), v) * (1.0 / totals)
            att_ref[:, at : at + HD] = att.astype(LOW)
            logs = jnp.where(lane == h, highest + jnp.log(totals), logs)
        log_ref[0] = logs.T[:8]

    def back_heads(self, own_ref, full_ref, log_ref, mask_ref, grad_att, out_ref, kind, pair_ref=None):
        cut = self.cut
        valid = mask_ref[...] > 0
        for h in range(self.heads):
            at = h * HD
            q = own_ref[0, :, at : at + HD] * LOW(HD ** (-0.5))
            k = full_ref[0, :, cut + at : cut + at + HD]
            v = full_ref[0, :, 2 * cut + at : 2 * cut + at + HD]
            grad = grad_att[:, at : at + HD]
            scores = jnp.where(valid, dot(k, q, ROWS), NEG_FILL)
            probs = jnp.exp(scores - log_ref[0, h : h + 1, :])
            products = probs * dot(v, grad, ROWS)
            inner = jnp.sum(products, axis=0, keepdims=True)
            grad_scores = (products - probs * inner).astype(LOW)
            grad_v = dot(probs.astype(LOW), grad).astype(kind)
            grad_k = dot(grad_scores, q).astype(kind)
            grad_q = (dot(grad_scores, k, DEEP) * HD ** (-0.5)).astype(LOW)
            if pair_ref is None:
                out_ref[0, :, at : at + HD] = grad_q
                out_ref[0, :, cut + at : cut + at + HD] = grad_k
                out_ref[0, :, 2 * cut + at : 2 * cut + at + HD] = grad_v
            else:
                out_ref[0, :, at : at + HD] = grad_q
                pair_ref[0, :, at : at + HD] = grad_k
                pair_ref[0, :, cut + at : cut + at + HD] = grad_v

    def attend(self, own, full, mask_row):
        cut, length, keys = self.cut, self.length, self.key_length

        def body(own_ref, full_ref, mask_ref, att_ref, log_ref):
            self.attend_heads(own_ref, full_ref, mask_ref, att_ref, log_ref)

        return call(
            body,
            (self.tensor,),
            [
                (own, pl.BlockSpec((1, length, 3 * cut), lambda j, *_: (j, 0, 0))),
                (full, pl.BlockSpec((1, keys, 3 * cut), lambda j, *_: (j, 0, 0))),
                whole(mask_row),
            ],
            [
                pl.BlockSpec((length, cut), lambda j: (0, j)),
                pl.BlockSpec((1, 8, length), lambda j, *_: (j, 0, 0)),
            ],
            [out((length, self.width), LOW), out((self.tensor, 8, length), FULL)],
            flops=16 * length * keys * self.width,
            size=16 * length * self.width,
        )

    def close_attention(self, attended, x, vectors, weights):
        cut, length, width = self.cut, self.length, self.width

        def body(scalars, att_ref, x_ref, vec_ref, *refs):
            w_refs = refs[: self.blocks]
            middle_ref, normed_ref = refs[self.blocks :]
            j = pl.program_id(0)

            @pl.when(j == 0)
            def _():
                middle_ref[...] = self.take_all(scalars, x_ref).astype(FULL) + vec_ref[2:3]

            middle_ref[...] += dot(att_ref[...], self.join(w_refs), ROWS)

            @pl.when(j == self.tensor - 1)
            def _():
                normal, _ = normalize(middle_ref[...])
                normed_ref[...] = (normal * vec_ref[3:4] + vec_ref[4:5]).astype(LOW)

        return call(
            body,
            (self.tensor,),
            [
                (attended, pl.BlockSpec((length, cut), lambda j, _: (0, j))),
                whole(x),
                whole(vectors),
            ]
            + self.weight_specs(weights, cut, lambda j, *_: (j, 0, 3)),
            [
                pl.BlockSpec((length, width), lambda j, _: (0, 0)),
                pl.BlockSpec((length, width), lambda j, _: (0, 0)),
            ],
            [out((length, width), FULL), out((length, width), LOW)],
            flops=2 * length * width * width,
            size=12 * length * width,
            scalars=self.scalars(),
        )

    def tile(self):
        return self.fan

    def expand(self, normed, row, weights, own_first):
        length, fan = self.length, self.fan
        total = fan * self.tensor

        def body(scalars, normed_ref, row_ref, *refs):
            w_refs = refs[: self.blocks]
            hidden_ref, slope_ref = refs[self.blocks :]
            before = dot(normed_ref[...], self.join(w_refs)) + row_ref[...]
            hidden, slope = gelu_parts(before)
            hidden_ref[...] = hidden.astype(LOW)
            slope_ref[...] = slope.astype(LOW)

        def row_map(j, s):
            return (0, self.group(s, j) if own_first else j)

        return call(
            body,
            (self.tensor,),
            [whole(normed), (row, pl.BlockSpec((1, fan), row_map))]
            + self.weight_specs(weights, fan, lambda j, *_: (j, 0, 0)),
            [pl.BlockSpec((length, fan), lambda j, _: (0, j))] * 2,
            [out((length, total), LOW)] * 2,
            flops=2 * length * self.width * total,
            size=4 * length * total,
            scalars=self.scalars(),
            room=14,
        )

    def reduce(self, hidden, middle, vectors, weights):
        length, width, tile = self.length, self.width, self.tile()
        per = self.fan // tile
        steps = self.tensor * per

        def body(scalars, hidden_ref, middle_ref, vec_ref, *refs):
            w_refs = refs[: self.blocks]
            out_ref, total = refs[self.blocks :]
            n = pl.program_id(0)

            @pl.when(n == 0)
            def _():
                total[...] = middle_ref[...] + vec_ref[5:6]

            total[...] += dot(hidden_ref[...], self.join(w_refs), ROWS)

            @pl.when(n == steps - 1)
            def _():
                self.put_all(scalars, out_ref, total[...].astype(LOW))

        return call(
            body,
            (steps,),
            [
                (hidden, pl.BlockSpec((length, tile), lambda n, _: (0, n))),
                whole(middle),
                whole(vectors),
            ]
            + self.weight_specs(weights, tile, lambda n, *_: (n // per, 0, n % per)),
            [pl.BlockSpec((length, width), lambda n, _: (0, 0))],
            [out((length, width), LOW)],
            [pltpu.VMEM((length, width), FULL)],
            flops=2 * length * width * self.fan * self.tensor,
            size=2 * length * self.fan * self.tensor,
            scalars=self.scalars(),
            room=14,
        )[0]

    def turn(self, scalars, ref, out_ref, plain=False):
        for o in range(self.blocks):
            at = o * self.depth
            block = self.take(scalars, ref, o) if plain else ref[:, at : at + self.depth]
            out_ref[at : at + self.depth, :] = block.T

    def put_halves(self, kept_ref, sent_ref, j, left, grad):
        count, columns = self.blocks // 2, grad.shape[1]
        rows = count * self.depth
        for ref, part in ((kept_ref, grad[:rows]), (sent_ref, grad[rows:])):
            ref[:, j, : self.depth, left : left + columns] = part.reshape(
                count, self.depth, columns
            )

    def weight_grad(self, left, rights, plain):
        length, depth, count = self.length, self.depth, self.blocks // 2
        pieces = [r.shape[2] if r.ndim == 3 else r.shape[1] // self.tensor for r in rights]
        columns = sum(pieces)

        def body(scalars, left_ref, *refs):
            r_refs = refs[: len(rights)]
            kept_ref, sent_ref, turned = refs[len(rights) :]

            @pl.when(pl.program_id(0) == 0)
            def _():
                self.turn(scalars, left_ref, turned, plain)

            at = 0
            for r, size in zip(r_refs, pieces, strict=True):
                right = r[0] if len(r.shape) == 3 else r[...]
                grad = dot(turned[...], right).astype(LOW)
                self.put_halves(kept_ref, sent_ref, 0, at, grad)
                at += size

        ins = [whole(left)]
        for r, size in zip(rights, pieces, strict=True):
            if r.ndim == 3:
                ins.append((r, pl.BlockSpec((1, length, size), lambda j, _: (j, 0, 0))))
            else:
                ins.append((r, pl.BlockSpec((length, size), lambda j, _: (0, j))))
        return call(
            body,
            (self.tensor,),
            ins,
            [pl.BlockSpec((count, 1, depth, columns), lambda j, _: (0, j, 0, 0))] * 2,
            [out((count, self.tensor, depth, columns), LOW)] * 2,
            [pltpu.VMEM((self.width, length), LOW)],
            flops=2 * length * self.width * columns * self.tensor,
            size=2 * self.width * columns * self.tensor,
            scalars=self.scalars(),
        )

    def feed_back(self, cotangent, slope, middle, vectors, reduces, expands):
        length, width, fan = self.length, self.width, self.fan

        def body(scalars, cot_ref, slope_ref, middle_ref, vec_ref, *refs):
            r_refs, e_refs = refs[: self.blocks], refs[self.blocks : 2 * self.blocks]
            full_ref, low_ref, sum_ref, row_ref, grad_ref, cot, total = refs[2 * self.blocks :]
            j = pl.program_id(0)

            @pl.when(j == 0)
            def _():
                cot[...] = self.take_all(scalars, cot_ref)
                total[...] = jnp.zeros_like(total)

            grad = dot(cot[...], self.join(r_refs)) * slope_ref[...].astype(FULL)
            grad = grad.astype(LOW)
            grad_ref[...] = grad
            row_ref[...] = jnp.sum(grad.astype(FULL), axis=0, keepdims=True)
            total[...] += dot(grad, self.join(e_refs), ROWS)

            @pl.when(j == self.tensor - 1)
            def _():
                grad = total[...]
                normal, scaling = normalize(middle_ref[...])
                grad_output = cot[...].astype(FULL)
                result = grad_output + norm_back(grad, normal, scaling, vec_ref[3:4])
                full_ref[...] = result
                low_ref[...] = result.astype(LOW)
                sum_ref[0:1] = jnp.sum(result, axis=0, keepdims=True)
                sum_ref[1:2] = jnp.sum(grad * normal, axis=0, keepdims=True)
                sum_ref[2:3] = jnp.sum(grad, axis=0, keepdims=True)
                sum_ref[3:4] = jnp.sum(grad_output, axis=0, keepdims=True)

        return call(
            body,
            (self.tensor,),
            [
                whole(cotangent),
                (slope, pl.BlockSpec((length, fan), lambda j, _: (0, j))),
                whole(middle),
                whole(vectors),
            ]
            + self.weight_specs(reduces, fan, lambda j, *_: (j, 0, 0))
            + self.weight_specs(expands, fan, lambda j, *_: (j, 0, 0)),
            [
                fixed((length, width)),
                fixed((length, width)),
                fixed((4, width)),
                pl.BlockSpec((1, fan), lambda j, _: (0, j)),
                pl.BlockSpec((length, fan), lambda j, _: (0, j)),
            ],
            [
                out((length, width), FULL),
                out((length, width), LOW),
                out((4, width), FULL),
                out((1, fan * self.tensor), FULL),
                out((length, fan * self.tensor), LOW),
            ],
            [pltpu.VMEM((length, width), LOW), pltpu.VMEM((length, width), FULL)],
            flops=4 * length * width * fan * self.tensor,
            size=16 * width * fan,
            scalars=self.scalars(),
            room=28,
        )

    def attend_back(self, own, full, logs, mask_column, grad_branch, weights, kind):
        cut, length, keys = self.cut, self.length, self.key_length

        def body(own_ref, full_ref, log_ref, mask_ref, branch_ref, *refs):
            w_refs = refs[: self.blocks]
            query_ref, pair_ref = refs[self.blocks :]
            grad_att = dot(branch_ref[...], self.join(w_refs)).astype(LOW)
            self.back_heads(
                own_ref, full_ref, log_ref, mask_ref, grad_att, query_ref, kind, pair_ref
            )

        return call(
            body,
            (self.tensor,),
            [
                (own, pl.BlockSpec((1, length, 3 * cut), lambda j, *_: (j, 0, 0))),
                (full, pl.BlockSpec((1, keys, 3 * cut), lambda j, *_: (j, 0, 0))),
                (logs, pl.BlockSpec((1, 8, length), lambda j, *_: (j, 0, 0))),
                whole(mask_column),
                whole(grad_branch),
            ]
            + self.weight_specs(weights, cut, lambda j, *_: (j, 0, 3)),
            [
                pl.BlockSpec((1, length, cut), lambda j, *_: (j, 0, 0)),
                pl.BlockSpec((1, keys, 2 * cut), lambda j, *_: (j, 0, 0)),
            ],
            [
                out((self.tensor, length, cut), LOW),
                out((self.tensor, keys, 2 * cut), kind),
            ],
            flops=40 * length * keys * self.width,
            size=20 * length * self.width,
        )

    def project_back(self, grad_query, grad_pair, x, grad_middle, vectors, weights):
        cut, length, width = self.cut, self.length, self.width

        def body(scalars, query_ref, pair_ref, x_ref, grad_ref, vec_ref, *refs):
            w_refs = refs[: self.blocks]
            out_ref, sum_ref, pair_sum_ref, total = refs[self.blocks :]
            j = pl.program_id(0)

            @pl.when(j == 0)
            def _():
                total[...] = jnp.zeros_like(total)

            query, pair = query_ref[0], pair_ref[0]
            total[...] += dot(query, self.join(w_refs, 0, cut), ROWS) + dot(
                pair, self.join(w_refs, cut, 3 * cut), ROWS
            )
            pair_sum_ref[0, :, :cut] = jnp.sum(query.astype(FULL), axis=0, keepdims=True)
            pair_sum_ref[0, :, cut:] = jnp.sum(pair.astype(FULL), axis=0, keepdims=True)

            @pl.when(j == self.tensor - 1)
            def _():
                grad = total[...]
                normal, scaling = normalize(self.take_all(scalars, x_ref).astype(FULL))
                result = grad_ref[...] + norm_back(grad, normal, scaling, vec_ref[0:1])
                self.put_all(scalars, out_ref, result.astype(LOW))
                sum_ref[0:1] = jnp.sum(grad * normal, axis=0, keepdims=True)
                sum_ref[1:2] = jnp.sum(grad, axis=0, keepdims=True)

        return call(
            body,
            (self.tensor,),
            [
                (grad_query, pl.BlockSpec((1, length, cut), lambda j, _: (j, 0, 0))),
                (grad_pair, pl.BlockSpec((1, length, 2 * cut), lambda j, _: (j, 0, 0))),
                whole(x),
                whole(grad_middle),
                whole(vectors),
            ]
            + self.weight_specs(weights, 4 * cut, lambda j, *_: (j, 0, 0)),
            [
                pl.BlockSpec((length, width), lambda j, _: (0, 0)),
                pl.BlockSpec((2, width), lambda j, _: (0, 0)),
                pl.BlockSpec((1, 1, 3 * cut), lambda j, _: (j, 0, 0)),
            ],
            [out((length, width), LOW), out((2, width), FULL), out((self.tensor, 1, 3 * cut), FULL)],
            [pltpu.VMEM((length, width), FULL)],
            flops=2 * length * width * 3 * cut * self.tensor,
            size=8 * length * width,
            scalars=self.scalars(),
        )

    def attention(self, x, mask_row, weights, start, count, before=None):
        cut, length, width, fan = self.cut, self.length, self.width, self.fan
        first, final = before is None, before is not None

        def body(scalars, x_ref, mask_ref, *refs):
            w_refs, refs = refs[: self.blocks], refs[self.blocks :]
            if first:
                own_ref, att_ref, log_ref, row_ref, middle_ref, normed_ref, vec_ref = refs[:7]
                refs = refs[7:]
            else:
                middle_in, normed_ref, vec_ref = refs[:3]
                own_ref, att_ref, log_ref, row_ref, middle_ref = refs[3:8]
                refs = refs[8:]
            j = pl.program_id(0)

            @pl.when(j == 0)
            def _():
                if first:
                    vectors = self.small_vectors(w_refs)
                    vec_ref[...] = vectors
                    rows = self.take_all(scalars, x_ref).astype(FULL)
                    middle_ref[...] = rows + vectors[2:3]
                    normal, _ = normalize(rows)
                    normed_ref[...] = (normal * vectors[0:1] + vectors[1:2]).astype(LOW)
                else:
                    middle_ref[...] = middle_in[...]

            bias, row_ref[...] = self.small_biases(w_refs)
            own = dot(normed_ref[...], self.join(w_refs, 0, 3 * cut)) + bias
            own_ref[0] = own.astype(LOW)
            self.attend_heads(own_ref, own_ref, mask_ref, att_ref, log_ref)
            middle_ref[...] += dot(att_ref[...], self.join(w_refs, 3 * cut, 4 * cut), ROWS)

            if final:
                (two_ref,) = refs

                @pl.when(j == count - 1)
                def _():
                    normal, _ = normalize(middle_ref[...])
                    two_ref[...] = (normal * vec_ref[3:4] + vec_ref[4:5]).astype(LOW)

        outs = [
            (pl.BlockSpec((1, length, 3 * cut), lambda j, _: (j, 0, 0)), out((count, length, 3 * cut), LOW)),
            (pl.BlockSpec((length, cut), lambda j, _: (0, j)), out((length, count * cut), LOW)),
            (pl.BlockSpec((1, 8, length), lambda j, _: (j, 0, 0)), out((count, 8, length), FULL)),
            (pl.BlockSpec((1, fan), lambda j, _: (0, j)), out((1, count * fan), FULL)),
            (fixed((length, width)), out((length, width), FULL)),
        ]
        if first:
            outs.append((fixed((length, width)), out((length, width), LOW)))
            outs.append((fixed((6, width)), out((6, width), FULL)))
        if final:
            outs.append((fixed((length, width)), out((length, width), LOW)))
        return call(
            body,
            (count,),
            [whole(x), whole(mask_row)]
            + self.weight_specs(weights, 4 * cut, lambda j, s: (self.group(s, start + j), 0, 0))
            + [whole(a) for a in before or ()],
            [spec for spec, _ in outs],
            [shape for _, shape in outs],
            flops=(8 * length * width * width + 4 * length * length * width) * count // self.tensor,
            size=16 * width * width,
            scalars=self.scalars(),
            room=20,
        )

    def attention_back(self, own, logs, mask_column, branch, weights, start, count, before=None, closing=None):
        cut, length, width = self.cut, self.length, self.width
        base = start % own.shape[0]
        first, final = before is None, closing is not None

        def body(scalars, own_ref, log_ref, mask_ref, branch_ref, *refs):
            w_refs, refs = refs[: self.blocks], refs[self.blocks :]
            if not first:
                (total_in,), refs = refs[:1], refs[1:]
            if final:
                (x_ref, grad_ref, vec_ref), refs = refs[:3], refs[3:]
                part_ref, pair_ref, out_ref, sum_ref, total = refs
            else:
                part_ref, pair_ref, total = refs
            j = pl.program_id(0)

            @pl.when(j == 0)
            def _():
                total[...] = jnp.zeros((length, width), FULL) if first else total_in[...]

            grad_att = dot(branch_ref[...], self.join(w_refs, 3 * cut, 4 * cut)).astype(LOW)
            self.back_heads(own_ref, own_ref, log_ref, mask_ref, grad_att, part_ref, LOW)
            grad = part_ref[0]
            total[...] += dot(grad, self.join(w_refs, 0, 3 * cut), ROWS)
            pair_ref[0] = jnp.sum(grad.astype(FULL), axis=0, keepdims=True)
            if final:

                @pl.when(j == count - 1)
                def _():
                    grad = total[...]
                    normal, scaling = normalize(self.take_all(scalars, x_ref).astype(FULL))
                    result = grad_ref[...] + norm_back(grad, normal, scaling, vec_ref[0:1])
                    self.put_all(scalars, out_ref, result.astype(LOW))
                    sum_ref[0:1] = jnp.sum(grad * normal, axis=0, keepdims=True)
                    sum_ref[1:2] = jnp.sum(grad, axis=0, keepdims=True)

        ins = [
            (own, pl.BlockSpec((1, length, 3 * cut), lambda j, _: (base + j, 0, 0))),
            (logs, pl.BlockSpec((1, 8, length), lambda j, _: (base + j, 0, 0))),
            whole(mask_column),
            whole(branch),
        ]
        ins += self.weight_specs(weights, 4 * cut, lambda j, s: (self.group(s, start + j), 0, 0))
        ins += [whole(a) for a in ((before,) if before is not None else ()) + (closing or ())]
        outs = [
            (pl.BlockSpec((1, length, 3 * cut), lambda j, _: (j, 0, 0)), out((count, length, 3 * cut), LOW)),
            (pl.BlockSpec((1, 1, 3 * cut), lambda j, _: (j, 0, 0)), out((count, 1, 3 * cut), FULL)),
            (fixed((length, width)), out((length, width), LOW if final else FULL)),
        ]
        if final:
            outs.append((fixed((2, width)), out((2, width), FULL)))
        return call(
            body,
            (count,),
            ins,
            [spec for spec, _ in outs],
            [shape for _, shape in outs],
            [pltpu.VMEM((length, width), FULL)] if final else [],
            flops=(8 * length * width * width + 10 * length * length * width) * count // self.tensor,
            size=32 * width * width,
            scalars=self.scalars(),
            room=24 if final else 18,
        )

    def first_grads(self, normed, branch, grads, attended, smalls=None):
        cut, length, width, depth = self.cut, self.length, self.width, self.depth
        count = attended.shape[1] // cut
        half, lanes = self.blocks // 2, 4 * self.cut
        times = 0 if smalls is None else self.tensor // count
        rows = depth + SMALL_ROWS * times
        smalls = list(smalls or ())

        def body(scalars, normed_ref, branch_ref, att_ref, *refs):
            parts, refs = refs[: len(grads)], refs[len(grads) :]
            kept_ref, sent_ref, turned, turned_two = refs[-4:]
            self.turn(scalars, normed_ref, turned)
            self.turn(scalars, branch_ref, turned_two)
            for j, (ref, k) in enumerate((r, k) for r in parts for k in range(r.shape[0])):
                self.put_halves(kept_ref, sent_ref, j, 0, dot(turned[...], ref[k]).astype(LOW))
                right = att_ref[:, j * cut : (j + 1) * cut]
                self.put_halves(
                    kept_ref, sent_ref, j, 3 * cut, dot(turned_two[...], right).astype(LOW)
                )
            if smalls:
                one_ref, two_ref, row_ref = refs[:3]
                pairs = [(r, k) for r in refs[3 : len(smalls)] for k in range(r.shape[0])]
                six = jnp.concatenate([one_ref[...], two_ref[...]], 0)
                for t, (ref, k) in enumerate(pairs):
                    sums = ref[k]
                    pair = jnp.concatenate([sums[:, :cut], sums[:, 2 * cut :]], 1)
                    at = self.group(scalars, t) * self.fan
                    row = row_ref[:, pl.ds(pl.multiple_of(at, self.fan), self.fan)]
                    at = depth + SMALL_ROWS * (t // count)
                    for o in range(self.blocks):
                        to = (kept_ref, sent_ref)[o // half]
                        to[o % half, t % count, at : at + SMALL_ROWS, :] = small_rows(
                            six[:, o * depth : (o + 1) * depth], pair, row, lanes
                        )

        return call(
            body,
            (1,),
            [whole(a) for a in [normed, branch, attended] + list(grads) + smalls],
            [fixed((half, count, rows, lanes))] * 2,
            [out((half, count, rows, lanes), LOW)] * 2,
            [pltpu.VMEM((width, length), LOW)] * 2,
            flops=8 * length * width * cut * count,
            size=2 * width * lanes * count,
            scalars=self.scalars(),
            room=24,
        )


class Layout:
    def __init__(self, sizes, images):
        self.dp, self.tensor = sizes["dp"], sizes["tensor"]
        self.images = images
        self.groups = self.tensor // images
        self.near = self.dp == 8
        self.me = lax.axis_index("dp")
        self.place = lax.axis_index("tensor")

    def swap(self, array, bit):
        return lax.ppermute(array, "dp", [(k, k ^ bit) for k in range(self.dp)])

    def swap_tensor(self, array, step):
        return lax.ppermute(array, "tensor", [(k, k ^ step) for k in range(self.tensor)])

    def spots(self):
        if not self.near:
            return None
        return jnp.array(ORDER, jnp.int32) ^ self.me.astype(jnp.int32)

    def ordered(self, array):
        if not self.near:
            return array
        return jnp.concatenate(
            [lax.dynamic_slice_in_dim(array, self.me ^ r, 1, 0) for r in ORDER], 0
        )

    def plain(self, array):
        if not self.near:
            return array
        pieces = []
        for block in range(8):
            r = self.me ^ block
            pieces.append(lax.dynamic_slice_in_dim(array, (r & 1) * 4 + (r >> 1), 1, 0))
        return jnp.concatenate(pieces, 0)

    def gather(self, shard, beside=None):
        line = lax.all_gather(shard, "tensor", axis=0)
        if beside is not None:
            line, beside[:] = lax.optimization_barrier((line, beside))
        if not self.near:
            return list(lax.all_gather(line, "dp", axis=0))
        half = self.tensor // 2
        by_x = self.swap(line, 2)
        by_y = self.swap(line, 4)
        top = self.swap(by_y[:half], 2)
        bottom = self.swap(by_x[half:], 4)
        far = jnp.concatenate([top, bottom], 0)
        mine = [line, by_x, by_y, far]
        return mine + [self.swap(block, 1) for block in mine]

    def scatter(self, kept, sent):
        if not self.near:
            return lax.psum_scatter(jnp.concatenate([kept, sent], 0), "dp", scatter_dimension=0)
        came = self.swap(sent, 1)
        half = kept.shape[1] // 2

        def add(*parts):
            return sum(part.astype(FULL) for part in parts).astype(LOW)

        top = self.swap(add(kept[3, :half], came[3, :half]), 2)
        bottom = self.swap(add(kept[3, half:], came[3, half:]), 4)
        x_block = jnp.concatenate(
            [add(kept[1, :half], came[1, :half]), add(kept[1, half:], came[1, half:], bottom)],
            0,
        )
        y_block = jnp.concatenate(
            [add(kept[2, :half], came[2, :half], top), add(kept[2, half:], came[2, half:])],
            0,
        )
        by_x = self.swap(x_block, 2)
        by_y = self.swap(y_block, 4)
        return add(kept[0], came[0], by_x, by_y)

    def scatter_line(self, total):
        total = lax.psum_scatter(total, "tensor", scatter_dimension=0)
        return total.astype(FULL)

    def scatter_near(self, near, far, lower):
        count = near.shape[0]
        total = near[0, :lower].astype(FULL)
        for step in range(1, count):
            total += self.swap_tensor(near[step, :lower], step).astype(FULL)
        for step in range(count, self.tensor):
            body = self.swap_tensor(far[step - count], step).astype(FULL)
            below = self.swap_tensor(near[step - count, lower:], step).astype(FULL)
            total += jnp.concatenate([body, below], 0)
        return total

    def split(self, array):
        spot = self.place % self.images
        return [
            lax.dynamic_index_in_dim(array, spot ^ step, 1, keepdims=False)
            for step in range(self.images)
        ]

    def to_image(self, blocks):
        came = [
            self.swap_tensor(block, step)
            for step, block in enumerate(blocks)
            if step
        ]
        return jnp.concatenate(blocks[:1] + came, 0)

    def from_image(self, array):
        spot = self.place % self.images
        rows = array.shape[0] // self.images
        blocks = [array[:rows]]
        for step in range(1, self.images):
            part = array[step * rows : (step + 1) * rows]
            blocks.append(self.swap_tensor(part, step))
        return jnp.stack(
            [self.pick(blocks, spot ^ image) for image in range(self.images)], 1
        )

    def pick(self, blocks, index):
        chosen = blocks[0]
        for k in range(1, len(blocks)):
            chosen = jnp.where(index == k, blocks[k], chosen)
        return chosen

    def halves(self, array):
        parts = [array]
        for group in range(1, self.groups):
            parts.append(self.swap_tensor(array, group * self.images))
        return parts[0] if len(parts) == 1 else jnp.concatenate(parts, 1)

    def halves_back(self, array):
        rows = array.shape[1] // self.groups
        total = array[:, :rows]
        for group in range(1, self.groups):
            total = total + self.swap_tensor(array[:, group * rows : (group + 1) * rows], group * self.images)
        return total.astype(LOW)

    def valid_keys(self, key_mask):
        rows = key_mask.shape[1] // self.tensor
        mine = lax.dynamic_index_in_dim(
            key_mask, self.place % self.images, 0, keepdims=False
        )
        return jnp.concatenate(
            [
                lax.dynamic_slice_in_dim(mine, (self.place ^ block) * rows, rows, 0)
                for block in range(self.tensor)
            ]
        )


def shards(
    sizes,
    tokens,
    attn_gain,
    attn_shift,
    qkv_weight,
    query_value_bias,
    proj_weight,
    proj_bias,
    mlp_gain,
    mlp_shift,
    expand_weight,
    expand_bias,
    reduce_weight,
    reduce_bias,
    key_mask,
    cotangent,
):
    lay = Layout(sizes, tokens.shape[1])
    depth = attn_gain.shape[0]
    cut = qkv_weight.shape[2]
    fan = expand_weight.shape[1]
    heads = cut // HD
    slots = query_value_bias.shape[2]
    length = tokens.shape[0] * lay.images
    keys = length * lay.groups
    do = Kernels(lay.dp, depth, lay.tensor, cut, fan, length, keys, lay.spots(), lay.place.astype(jnp.int32))

    token_blocks, cot_blocks = lay.split(tokens), lay.split(cotangent)
    lanes, count = 4 * cut, expand_bias.size
    six = jnp.stack([attn_gain, attn_shift, proj_bias, mlp_gain, mlp_shift, reduce_bias]).astype(FULL)
    owner = jnp.arange(lay.dp)[:, None] == lay.me
    pair = jnp.where(owner, query_value_bias.astype(FULL)[:, :, None], 0.0).reshape(1, -1)
    row = jnp.where(owner, expand_bias.astype(FULL), 0.0).reshape(1, -1)
    first, turned = do.pack(qkv_weight.transpose(1, 0, 2), proj_weight, reduce_weight, six, pair, row)
    beside = token_blocks + cot_blocks
    first_blocks = lay.gather(first, beside)
    token_blocks, cot_blocks = beside[: lay.images], beside[lay.images :]
    image = lay.to_image(token_blocks)
    expand_blocks = lay.gather(expand_weight)
    reduce_blocks = lay.gather(turned)
    cot_image = lay.to_image(cot_blocks)
    mask = lay.valid_keys(key_mask)

    together = lay.groups == 1
    if together:
        split = lay.tensor // 2
        own_two, attended_two, logs_two, row_two, middle, normed_one, vectors = do.attention(
            image, mask[None], first_blocks, split, split
        )
        own, attended, logs, row, middle, normed_two = do.attention(
            image, mask[None], first_blocks, 0, split, (middle, normed_one, vectors)
        )
        expand_row = jnp.concatenate([row, row_two], 1)
    else:
        normed_one, own, vectors, expand_row = do.project(image, first_blocks)
        full = lay.halves(own)
        attended, logs = do.attend(own, full, mask[None])
        middle, normed_two = do.close_attention(attended, image, vectors, first_blocks)
    hidden, slope = do.expand(normed_two, expand_row, expand_blocks, together)
    block_output = lay.from_image(do.reduce(hidden, middle, vectors, reduce_blocks))

    halves = do.weight_grad(cot_image, [hidden], True)
    reduce_grad = lay.scatter_line(lay.scatter(*halves)).T
    grad_middle, grad_branch, sums, row_grad, grad_before = do.feed_back(
        cot_image, slope, middle, vectors, reduce_blocks, expand_blocks
    )
    halves = do.weight_grad(normed_two, [grad_before], False)
    expand_grad = lay.scatter_line(lay.scatter(*halves))
    if together:
        column = mask[:, None]
        grads, pairs, total = do.attention_back(
            own_two, logs_two, column, grad_branch, first_blocks, split, split
        )
        halves = do.first_grads(normed_one, grad_branch, [grads], attended_two)
        far = lay.scatter(*halves)
        grads, pairs = [], [pairs]
        for start in range(split - 1, 0, -1):
            grad, pair, total = do.attention_back(
                own, logs, column, grad_branch, first_blocks, start, 1, total
            )
            grads, pairs = [grad] + grads, [pair] + pairs
        grad, pair, tokens_grad, sums_one = do.attention_back(
            own, logs, column, grad_branch, first_blocks, 0, 1, total, (image, grad_middle, vectors)
        )
        halves = do.first_grads(
            normed_one, grad_branch, [grad] + grads, attended, [sums_one, sums, row_grad, pair] + pairs
        )
        near = lay.scatter(*halves)
        last = lay.scatter_near(near, far, depth + SMALL_ROWS)
    else:
        grad_query, grad_pair = do.attend_back(
            own, full, logs, mask[:, None], grad_branch, first_blocks, FULL
        )
        grad_pair = lay.halves_back(grad_pair)
        tokens_grad, sums_one, pair_sums = do.project_back(
            grad_query, grad_pair, image, grad_middle, vectors, first_blocks
        )
        qkv_halves = do.weight_grad(normed_one, [grad_query, grad_pair], False)
        proj_halves = do.weight_grad(grad_branch, [attended], False)
        six = jnp.concatenate([sums_one, sums], 0)
        pair_rows = jnp.concatenate([pair_sums[:, 0, :cut], pair_sums[:, 0, 2 * cut :]], 1)
        rows = jnp.stack(
            [
                jnp.stack(
                    [
                        small_rows(
                            six[:, o * depth : (o + 1) * depth],
                            pair_rows[t : t + 1],
                            row_grad[:, t * fan : (t + 1) * fan],
                            lanes,
                        )
                        for t in range(lay.tensor)
                    ]
                )
                for o in range(lay.dp)
            ]
        )
        half = lay.dp // 2
        halves = [
            jnp.concatenate([jnp.concatenate([qkv, proj], 3), small], 2)
            for qkv, proj, small in zip(qkv_halves, proj_halves, (rows[:half], rows[half:]), strict=True)
        ]
        last = lay.scatter_line(lay.scatter(*halves))
    tokens_grad = lay.from_image(tokens_grad)
    vector_grads = last[depth, : 6 * depth].reshape(6, depth)
    pair_grad = last[depth + 1, : 2 * cut].reshape(2, heads, HD)
    pair_grad = lax.dynamic_slice_in_dim(pair_grad, lay.me * slots, slots, 2)
    row_part = lax.dynamic_slice_in_dim(last[depth + 2], lay.me * count, count, 0)
    return (
        block_output,
        tokens_grad,
        vector_grads[0],
        vector_grads[1],
        last[:depth, : 3 * cut].reshape(depth, 3, cut),
        pair_grad,
        last[:depth, 3 * cut :].T,
        vector_grads[2],
        vector_grads[3],
        vector_grads[4],
        expand_grad,
        row_part.reshape(expand_bias.shape),
        reduce_grad,
        vector_grads[5],
    )


def solution(mesh):
    placed = (
        P("tensor", "dp", None),
        P("dp"),
        P("dp"),
        P("dp", None, "tensor"),
        P(None, "tensor", "dp"),
        P("tensor", "dp"),
        P("dp"),
        P("dp"),
        P("dp"),
        P("dp", "tensor"),
        P("tensor", "dp"),
        P("tensor", "dp"),
        P("dp"),
        P("dp", None),
        P("tensor", "dp", None),
    )

    def step(*arrays):
        return shards(dict(mesh.shape), *arrays)

    return jax.shard_map(
        step,
        mesh=mesh,
        in_specs=placed,
        out_specs=(
            P("tensor", "dp", None),
            P("tensor", "dp", None),
            P("dp"),
            P("dp"),
            P("dp", None, "tensor"),
            P(None, "tensor", "dp"),
            P("tensor", "dp"),
            P("dp"),
            P("dp"),
            P("dp"),
            P("dp", "tensor"),
            P("tensor", "dp"),
            P("tensor", "dp"),
            P("dp"),
        ),
        check_vma=False,
    )
```

```python
import jax
import jax.numpy as jnp
from jax import lax
from jax.experimental import pallas as pl
from jax.experimental.pallas import tpu as pltpu
from jax.sharding import PartitionSpec as P

HD = 64
EPSILON = 1e-06
NEG_FILL = -1e30
LOW = jnp.bfloat16
FULL = jnp.float32
ORDER = (0, 2, 4, 6, 1, 3, 5, 7)
SMALL_ROWS = 16
MIB = 1024 * 1024
ROWS = (((1,), (1,)), ((), ()))
PLAIN = (((1,), (0,)), ((), ()))
DEEP = (((0,), (0,)), ((), ()))


def dot(left, right, contract=PLAIN):
    return lax.dot_general(left, right, contract, preferred_element_type=FULL)


def normalize(rows):
    average = jnp.mean(rows, axis=-1, keepdims=True)
    centered = rows - average
    variance = jnp.mean(centered * centered, axis=-1, keepdims=True)
    scaling = lax.rsqrt(variance + EPSILON)
    return centered * scaling, scaling


def norm_back(grad_output, normal, scaling, gain):
    grad_normal = grad_output * gain
    first_mean = jnp.mean(grad_normal, axis=-1, keepdims=True)
    second_mean = jnp.mean(grad_normal * normal, axis=-1, keepdims=True)
    return scaling * (grad_normal - first_mean - normal * second_mean)


def gelu_parts(v):
    t = 1.0 / (1.0 + 0.23164189 * jnp.abs(v))
    bell = jnp.exp2(v * v * -0.7213475204444817)
    poly = 0.127414796 + t * (
        -0.142248368 + t * (0.7107068705 + t * (-0.7265760135 + t * 0.5307027145))
    )
    tail = poly * (t * bell)
    phi = jnp.where(v < 0.0, tail, 1.0 - tail)
    return v * phi, phi + (v * 0.3989422804014327) * bell


def small_rows(six, pair, row, lanes):
    def wide(values):
        pad = lanes - values.shape[1]
        return jnp.pad(values, ((0, 0), (0, pad))) if pad else values

    first = wide(jnp.concatenate([six[k : k + 1] for k in range(6)], 1))
    at = lax.broadcasted_iota(jnp.int32, (SMALL_ROWS, lanes), 0)
    rows = jnp.where(at == 0, first, jnp.where(at == 1, wide(pair), jnp.where(at == 2, wide(row), 0.0)))
    return rows.astype(LOW)


def call(body, grid, ins, outs, shapes, scratch=(), flops=0, size=0, scalars=None, room=12):
    spec = pltpu.PrefetchScalarGridSpec(
        num_scalar_prefetch=0 if scalars is None else 1,
        grid=grid,
        in_specs=[s for _, s in ins],
        out_specs=outs,
        scratch_shapes=list(scratch),
    )
    operands = [a for a, _ in ins]
    if scalars is not None:
        operands = [scalars] + operands
    return pl.pallas_call(
        body,
        grid_spec=spec,
        out_shape=shapes,
        cost_estimate=pl.CostEstimate(flops=flops, bytes_accessed=size, transcendentals=0),
        compiler_params=pltpu.CompilerParams(vmem_limit_bytes=room * MIB),
    )(*operands)


def whole(array):
    zeros = (0,) * array.ndim
    return array, pl.BlockSpec(array.shape, lambda *_: zeros, pipeline_mode=pl.Buffered(1))


def fixed(shape):
    zeros = (0,) * len(shape)
    return pl.BlockSpec(shape, lambda *_: zeros)


def out(shape, kind):
    return jax.ShapeDtypeStruct(shape, kind)


class Kernels:
    def __init__(self, blocks, depth, tensor, cut, fan, length, key_length, spots, place):
        self.blocks, self.depth, self.tensor = blocks, depth, tensor
        self.cut, self.fan, self.length, self.key_length = cut, fan, length, key_length
        self.width = blocks * depth
        self.spots = spots
        self.place = place
        self.heads = cut // HD

    def take(self, scalars, ref, o):
        if self.spots is None:
            return ref[:, o * self.depth : (o + 1) * self.depth]
        return ref[:, pl.ds(pl.multiple_of(scalars[o] * self.depth, self.depth), self.depth)]

    def take_all(self, scalars, ref):
        if self.spots is None:
            return ref[...]
        return jnp.concatenate([self.take(scalars, ref, o) for o in range(self.blocks)], 1)

    def put_all(self, scalars, ref, value):
        if self.spots is None:
            ref[...] = value
        else:
            for o in range(self.blocks):
                ref[:, pl.ds(pl.multiple_of(scalars[o] * self.depth, self.depth), self.depth)] = (
                    value[:, o * self.depth : (o + 1) * self.depth]
                )

    def scalars(self):
        spots = jnp.arange(self.blocks, dtype=jnp.int32) if self.spots is None else self.spots
        return jnp.concatenate([spots, self.place[None]])

    def group(self, scalars, t):
        return t ^ scalars[self.blocks]

    def weight_specs(self, arrays, columns, index):
        return [
            (
                pltpu.with_memory_space_constraint(a, pltpu.HBM),
                pl.BlockSpec((1, a.shape[1], columns), lambda *g, index=index: index(*g)),
            )
            for a in arrays
        ]

    def join(self, refs, left=0, right=None):
        right = refs[0].shape[2] if right is None else right
        return jnp.concatenate([r[0, : self.depth, left:right] for r in refs], 0)

    def pack(self, qkv, proj, reduce, six, pair, row):
        cut, depth, fan = self.cut, self.depth, self.fan

        def body(qkv_ref, proj_ref, reduce_ref, six_ref, pair_ref, row_ref, first_ref, turned_ref):
            for c in range(3):
                first_ref[:depth, c * cut : (c + 1) * cut] = qkv_ref[c]
            first_ref[:depth, 3 * cut :] = proj_ref[...].T
            first_ref[depth:, :] = small_rows(six_ref[...], pair_ref[...], row_ref[...], 4 * cut)
            turned_ref[...] = reduce_ref[...].T

        return call(
            body,
            (1,),
            [whole(a) for a in (qkv, proj, reduce, six, pair, row)],
            [fixed((depth + SMALL_ROWS, 4 * cut)), fixed((depth, fan))],
            [out((depth + SMALL_ROWS, 4 * cut), LOW), out((depth, fan), LOW)],
            size=8 * depth * fan,
            room=4,
        )

    def small_vectors(self, refs):
        depth = self.depth
        rows = [r[0, depth : depth + 8, :].astype(FULL)[0:1] for r in refs]
        return jnp.concatenate(
            [
                jnp.concatenate([row[:, k * depth : (k + 1) * depth] for row in rows], 1)
                for k in range(6)
            ],
            0,
        )

    def small_biases(self, refs):
        cut, depth = self.cut, self.depth
        rows = sum(r[0, depth : depth + 8, :].astype(FULL) for r in refs)
        pair = rows[1:2]
        bias = jnp.concatenate([pair[:, :cut], jnp.zeros((1, cut), FULL), pair[:, cut : 2 * cut]], 1)
        return bias, rows[2:3]

    def project(self, x, weights):
        cut, length, width, fan = self.cut, self.length, self.width, self.fan

        def body(scalars, x_ref, *refs):
            w_refs = refs[: self.blocks]
            normed_ref, proj_ref, vec_ref, row_ref = refs[self.blocks :]

            @pl.when(pl.program_id(0) == 0)
            def _():
                vectors = self.small_vectors(w_refs)
                vec_ref[...] = vectors
                normal, _ = normalize(self.take_all(scalars, x_ref).astype(FULL))
                normed_ref[...] = (normal * vectors[0:1] + vectors[1:2]).astype(LOW)

            bias, row_ref[...] = self.small_biases(w_refs)
            proj = dot(normed_ref[...], self.join(w_refs, 0, 3 * cut)) + bias
            proj_ref[0] = proj.astype(LOW)

        return call(
            body,
            (self.tensor,),
            [whole(x)] + self.weight_specs(weights, 4 * cut, lambda j, *_: (j, 0, 0)),
            [
                fixed((length, width)),
                pl.BlockSpec((1, length, 3 * cut), lambda j, _: (j, 0, 0)),
                fixed((6, width)),
                pl.BlockSpec((1, fan), lambda j, _: (0, j)),
            ],
            [
                out((length, width), LOW),
                out((self.tensor, length, 3 * cut), LOW),
                out((6, width), FULL),
                out((1, fan * self.tensor), FULL),
            ],
            flops=2 * length * width * 3 * cut * self.tensor,
            size=16 * width * width,
            scalars=self.scalars(),
        )

    def attend_heads(self, own_ref, full_ref, mask_ref, att_ref, log_ref):
        cut, length = self.cut, self.length
        valid = mask_ref[...] > 0
        lane = lax.broadcasted_iota(jnp.int32, (length, 128), 1)
        logs = jnp.zeros((length, 128), FULL)
        for h in range(self.heads):
            at = h * HD
            q = own_ref[0, :, at : at + HD] * LOW(HD ** (-0.5))
            k = full_ref[0, :, cut + at : cut + at + HD]
            v = full_ref[0, :, 2 * cut + at : 2 * cut + at + HD]
            scores = jnp.where(valid, dot(q, k, ROWS), NEG_FILL)
            highest = jnp.max(scores, axis=-1, keepdims=True)
            expanded = jnp.exp(scores - highest)
            totals = jnp.sum(expanded, axis=-1, keepdims=True)
            att = dot(expanded.astype(LOW), v) * (1.0 / totals)
            att_ref[:, at : at + HD] = att.astype(LOW)
            logs = jnp.where(lane == h, highest + jnp.log(totals), logs)
        log_ref[0] = logs.T[:8]

    def back_heads(self, own_ref, full_ref, log_ref, mask_ref, grad_att, out_ref, kind, pair_ref=None):
        cut = self.cut
        valid = mask_ref[...] > 0
        for h in range(self.heads):
            at = h * HD
            q = own_ref[0, :, at : at + HD] * LOW(HD ** (-0.5))
            k = full_ref[0, :, cut + at : cut + at + HD]
            v = full_ref[0, :, 2 * cut + at : 2 * cut + at + HD]
            grad = grad_att[:, at : at + HD]
            scores = jnp.where(valid, dot(k, q, ROWS), NEG_FILL)
            probs = jnp.exp(scores - log_ref[0, h : h + 1, :])
            products = probs * dot(v, grad, ROWS)
            inner = jnp.sum(products, axis=0, keepdims=True)
            grad_scores = (products - probs * inner).astype(LOW)
            grad_v = dot(probs.astype(LOW), grad).astype(kind)
            grad_k = dot(grad_scores, q).astype(kind)
            grad_q = (dot(grad_scores, k, DEEP) * HD ** (-0.5)).astype(LOW)
            if pair_ref is None:
                out_ref[0, :, at : at + HD] = grad_q
                out_ref[0, :, cut + at : cut + at + HD] = grad_k
                out_ref[0, :, 2 * cut + at : 2 * cut + at + HD] = grad_v
            else:
                out_ref[0, :, at : at + HD] = grad_q
                pair_ref[0, :, at : at + HD] = grad_k
                pair_ref[0, :, cut + at : cut + at + HD] = grad_v

    def attend(self, own, full, mask_row):
        cut, length, keys = self.cut, self.length, self.key_length

        def body(own_ref, full_ref, mask_ref, att_ref, log_ref):
            self.attend_heads(own_ref, full_ref, mask_ref, att_ref, log_ref)

        return call(
            body,
            (self.tensor,),
            [
                (own, pl.BlockSpec((1, length, 3 * cut), lambda j, *_: (j, 0, 0))),
                (full, pl.BlockSpec((1, keys, 3 * cut), lambda j, *_: (j, 0, 0))),
                whole(mask_row),
            ],
            [
                pl.BlockSpec((length, cut), lambda j: (0, j)),
                pl.BlockSpec((1, 8, length), lambda j, *_: (j, 0, 0)),
            ],
            [out((length, self.width), LOW), out((self.tensor, 8, length), FULL)],
            flops=16 * length * keys * self.width,
            size=16 * length * self.width,
        )

    def close_attention(self, attended, x, vectors, weights):
        cut, length, width = self.cut, self.length, self.width

        def body(scalars, att_ref, x_ref, vec_ref, *refs):
            w_refs = refs[: self.blocks]
            middle_ref, normed_ref = refs[self.blocks :]
            j = pl.program_id(0)

            @pl.when(j == 0)
            def _():
                middle_ref[...] = self.take_all(scalars, x_ref).astype(FULL) + vec_ref[2:3]

            middle_ref[...] += dot(att_ref[...], self.join(w_refs), ROWS)

            @pl.when(j == self.tensor - 1)
            def _():
                normal, _ = normalize(middle_ref[...])
                normed_ref[...] = (normal * vec_ref[3:4] + vec_ref[4:5]).astype(LOW)

        return call(
            body,
            (self.tensor,),
            [
                (attended, pl.BlockSpec((length, cut), lambda j, _: (0, j))),
                whole(x),
                whole(vectors),
            ]
            + self.weight_specs(weights, cut, lambda j, *_: (j, 0, 3)),
            [
                pl.BlockSpec((length, width), lambda j, _: (0, 0)),
                pl.BlockSpec((length, width), lambda j, _: (0, 0)),
            ],
            [out((length, width), FULL), out((length, width), LOW)],
            flops=2 * length * width * width,
            size=12 * length * width,
            scalars=self.scalars(),
        )

    def tile(self):
        return self.fan

    def expand(self, normed, row, weights, own_first):
        length, fan = self.length, self.fan
        total = fan * self.tensor

        def body(scalars, normed_ref, row_ref, *refs):
            w_refs = refs[: self.blocks]
            hidden_ref, slope_ref = refs[self.blocks :]
            before = dot(normed_ref[...], self.join(w_refs)) + row_ref[...]
            hidden, slope = gelu_parts(before)
            hidden_ref[...] = hidden.astype(LOW)
            slope_ref[...] = slope.astype(LOW)

        def row_map(j, s):
            return (0, self.group(s, j) if own_first else j)

        return call(
            body,
            (self.tensor,),
            [whole(normed), (row, pl.BlockSpec((1, fan), row_map))]
            + self.weight_specs(weights, fan, lambda j, *_: (j, 0, 0)),
            [pl.BlockSpec((length, fan), lambda j, _: (0, j))] * 2,
            [out((length, total), LOW)] * 2,
            flops=2 * length * self.width * total,
            size=4 * length * total,
            scalars=self.scalars(),
            room=14,
        )

    def reduce(self, hidden, middle, vectors, weights):
        length, width, tile = self.length, self.width, self.tile()
        per = self.fan // tile
        steps = self.tensor * per

        def body(scalars, hidden_ref, middle_ref, vec_ref, *refs):
            w_refs = refs[: self.blocks]
            out_ref, total = refs[self.blocks :]
            n = pl.program_id(0)

            @pl.when(n == 0)
            def _():
                total[...] = middle_ref[...] + vec_ref[5:6]

            total[...] += dot(hidden_ref[...], self.join(w_refs), ROWS)

            @pl.when(n == steps - 1)
            def _():
                self.put_all(scalars, out_ref, total[...].astype(LOW))

        return call(
            body,
            (steps,),
            [
                (hidden, pl.BlockSpec((length, tile), lambda n, _: (0, n))),
                whole(middle),
                whole(vectors),
            ]
            + self.weight_specs(weights, tile, lambda n, *_: (n // per, 0, n % per)),
            [pl.BlockSpec((length, width), lambda n, _: (0, 0))],
            [out((length, width), LOW)],
            [pltpu.VMEM((length, width), FULL)],
            flops=2 * length * width * self.fan * self.tensor,
            size=2 * length * self.fan * self.tensor,
            scalars=self.scalars(),
            room=14,
        )[0]

    def turn(self, scalars, ref, out_ref, plain=False):
        for o in range(self.blocks):
            at = o * self.depth
            block = self.take(scalars, ref, o) if plain else ref[:, at : at + self.depth]
            out_ref[at : at + self.depth, :] = block.T

    def put_halves(self, kept_ref, sent_ref, j, left, grad):
        count, columns = self.blocks // 2, grad.shape[1]
        rows = count * self.depth
        for ref, part in ((kept_ref, grad[:rows]), (sent_ref, grad[rows:])):
            ref[:, j, : self.depth, left : left + columns] = part.reshape(
                count, self.depth, columns
            )

    def weight_grad(self, left, rights, plain):
        length, depth, count = self.length, self.depth, self.blocks // 2
        pieces = [r.shape[2] if r.ndim == 3 else r.shape[1] // self.tensor for r in rights]
        columns = sum(pieces)

        def body(scalars, left_ref, *refs):
            r_refs = refs[: len(rights)]
            kept_ref, sent_ref, turned = refs[len(rights) :]

            @pl.when(pl.program_id(0) == 0)
            def _():
                self.turn(scalars, left_ref, turned, plain)

            at = 0
            for r, size in zip(r_refs, pieces, strict=True):
                right = r[0] if len(r.shape) == 3 else r[...]
                grad = dot(turned[...], right).astype(LOW)
                self.put_halves(kept_ref, sent_ref, 0, at, grad)
                at += size

        ins = [whole(left)]
        for r, size in zip(rights, pieces, strict=True):
            if r.ndim == 3:
                ins.append((r, pl.BlockSpec((1, length, size), lambda j, _: (j, 0, 0))))
            else:
                ins.append((r, pl.BlockSpec((length, size), lambda j, _: (0, j))))
        return call(
            body,
            (self.tensor,),
            ins,
            [pl.BlockSpec((count, 1, depth, columns), lambda j, _: (0, j, 0, 0))] * 2,
            [out((count, self.tensor, depth, columns), LOW)] * 2,
            [pltpu.VMEM((self.width, length), LOW)],
            flops=2 * length * self.width * columns * self.tensor,
            size=2 * self.width * columns * self.tensor,
            scalars=self.scalars(),
        )

    def feed_back(self, cotangent, slope, middle, vectors, reduces, expands):
        length, width, fan = self.length, self.width, self.fan

        def body(scalars, cot_ref, slope_ref, middle_ref, vec_ref, *refs):
            r_refs, e_refs = refs[: self.blocks], refs[self.blocks : 2 * self.blocks]
            full_ref, low_ref, sum_ref, row_ref, grad_ref, cot, total = refs[2 * self.blocks :]
            j = pl.program_id(0)

            @pl.when(j == 0)
            def _():
                cot[...] = self.take_all(scalars, cot_ref)
                total[...] = jnp.zeros_like(total)

            grad = dot(cot[...], self.join(r_refs)) * slope_ref[...].astype(FULL)
            grad = grad.astype(LOW)
            grad_ref[...] = grad
            row_ref[...] = jnp.sum(grad.astype(FULL), axis=0, keepdims=True)
            total[...] += dot(grad, self.join(e_refs), ROWS)

            @pl.when(j == self.tensor - 1)
            def _():
                grad = total[...]
                normal, scaling = normalize(middle_ref[...])
                grad_output = cot[...].astype(FULL)
                result = grad_output + norm_back(grad, normal, scaling, vec_ref[3:4])
                full_ref[...] = result
                low_ref[...] = result.astype(LOW)
                sum_ref[0:1] = jnp.sum(result, axis=0, keepdims=True)
                sum_ref[1:2] = jnp.sum(grad * normal, axis=0, keepdims=True)
                sum_ref[2:3] = jnp.sum(grad, axis=0, keepdims=True)
                sum_ref[3:4] = jnp.sum(grad_output, axis=0, keepdims=True)

        return call(
            body,
            (self.tensor,),
            [
                whole(cotangent),
                (slope, pl.BlockSpec((length, fan), lambda j, _: (0, j))),
                whole(middle),
                whole(vectors),
            ]
            + self.weight_specs(reduces, fan, lambda j, *_: (j, 0, 0))
            + self.weight_specs(expands, fan, lambda j, *_: (j, 0, 0)),
            [
                fixed((length, width)),
                fixed((length, width)),
                fixed((4, width)),
                pl.BlockSpec((1, fan), lambda j, _: (0, j)),
                pl.BlockSpec((length, fan), lambda j, _: (0, j)),
            ],
            [
                out((length, width), FULL),
                out((length, width), LOW),
                out((4, width), FULL),
                out((1, fan * self.tensor), FULL),
                out((length, fan * self.tensor), LOW),
            ],
            [pltpu.VMEM((length, width), LOW), pltpu.VMEM((length, width), FULL)],
            flops=4 * length * width * fan * self.tensor,
            size=16 * width * fan,
            scalars=self.scalars(),
            room=28,
        )

    def attend_back(self, own, full, logs, mask_column, grad_branch, weights, kind):
        cut, length, keys = self.cut, self.length, self.key_length

        def body(own_ref, full_ref, log_ref, mask_ref, branch_ref, *refs):
            w_refs = refs[: self.blocks]
            query_ref, pair_ref = refs[self.blocks :]
            grad_att = dot(branch_ref[...], self.join(w_refs)).astype(LOW)
            self.back_heads(
                own_ref, full_ref, log_ref, mask_ref, grad_att, query_ref, kind, pair_ref
            )

        return call(
            body,
            (self.tensor,),
            [
                (own, pl.BlockSpec((1, length, 3 * cut), lambda j, *_: (j, 0, 0))),
                (full, pl.BlockSpec((1, keys, 3 * cut), lambda j, *_: (j, 0, 0))),
                (logs, pl.BlockSpec((1, 8, length), lambda j, *_: (j, 0, 0))),
                whole(mask_column),
                whole(grad_branch),
            ]
            + self.weight_specs(weights, cut, lambda j, *_: (j, 0, 3)),
            [
                pl.BlockSpec((1, length, cut), lambda j, *_: (j, 0, 0)),
                pl.BlockSpec((1, keys, 2 * cut), lambda j, *_: (j, 0, 0)),
            ],
            [
                out((self.tensor, length, cut), LOW),
                out((self.tensor, keys, 2 * cut), kind),
            ],
            flops=40 * length * keys * self.width,
            size=20 * length * self.width,
        )

    def project_back(self, grad_query, grad_pair, x, grad_middle, vectors, weights):
        cut, length, width = self.cut, self.length, self.width

        def body(scalars, query_ref, pair_ref, x_ref, grad_ref, vec_ref, *refs):
            w_refs = refs[: self.blocks]
            out_ref, sum_ref, pair_sum_ref, total = refs[self.blocks :]
            j = pl.program_id(0)

            @pl.when(j == 0)
            def _():
                total[...] = jnp.zeros_like(total)

            query, pair = query_ref[0], pair_ref[0]
            total[...] += dot(query, self.join(w_refs, 0, cut), ROWS) + dot(
                pair, self.join(w_refs, cut, 3 * cut), ROWS
            )
            pair_sum_ref[0, :, :cut] = jnp.sum(query.astype(FULL), axis=0, keepdims=True)
            pair_sum_ref[0, :, cut:] = jnp.sum(pair.astype(FULL), axis=0, keepdims=True)

            @pl.when(j == self.tensor - 1)
            def _():
                grad = total[...]
                normal, scaling = normalize(self.take_all(scalars, x_ref).astype(FULL))
                result = grad_ref[...] + norm_back(grad, normal, scaling, vec_ref[0:1])
                self.put_all(scalars, out_ref, result.astype(LOW))
                sum_ref[0:1] = jnp.sum(grad * normal, axis=0, keepdims=True)
                sum_ref[1:2] = jnp.sum(grad, axis=0, keepdims=True)

        return call(
            body,
            (self.tensor,),
            [
                (grad_query, pl.BlockSpec((1, length, cut), lambda j, _: (j, 0, 0))),
                (grad_pair, pl.BlockSpec((1, length, 2 * cut), lambda j, _: (j, 0, 0))),
                whole(x),
                whole(grad_middle),
                whole(vectors),
            ]
            + self.weight_specs(weights, 4 * cut, lambda j, *_: (j, 0, 0)),
            [
                pl.BlockSpec((length, width), lambda j, _: (0, 0)),
                pl.BlockSpec((2, width), lambda j, _: (0, 0)),
                pl.BlockSpec((1, 1, 3 * cut), lambda j, _: (j, 0, 0)),
            ],
            [out((length, width), LOW), out((2, width), FULL), out((self.tensor, 1, 3 * cut), FULL)],
            [pltpu.VMEM((length, width), FULL)],
            flops=2 * length * width * 3 * cut * self.tensor,
            size=8 * length * width,
            scalars=self.scalars(),
        )

    def attention(self, x, mask_row, weights, count, before=None):
        cut, length, width, fan = self.cut, self.length, self.width, self.fan
        first, final = before is None, before is not None

        def body(scalars, x_ref, mask_ref, *refs):
            w_refs, refs = refs[: self.blocks], refs[self.blocks :]
            if first:
                own_ref, att_ref, log_ref, row_ref, middle_ref, normed_ref, vec_ref = refs[:7]
                refs = refs[7:]
            else:
                middle_in, normed_ref, vec_ref = refs[:3]
                own_ref, att_ref, log_ref, row_ref, middle_ref = refs[3:8]
                refs = refs[8:]
            j = pl.program_id(0)

            @pl.when(j == 0)
            def _():
                if first:
                    vectors = self.small_vectors(w_refs)
                    vec_ref[...] = vectors
                    rows = self.take_all(scalars, x_ref).astype(FULL)
                    middle_ref[...] = rows + vectors[2:3]
                    normal, _ = normalize(rows)
                    normed_ref[...] = (normal * vectors[0:1] + vectors[1:2]).astype(LOW)
                else:
                    middle_ref[...] = middle_in[...]

            bias, row_ref[...] = self.small_biases(w_refs)
            own = dot(normed_ref[...], self.join(w_refs, 0, 3 * cut)) + bias
            own_ref[0] = own.astype(LOW)
            self.attend_heads(own_ref, own_ref, mask_ref, att_ref, log_ref)
            middle_ref[...] += dot(att_ref[...], self.join(w_refs, 3 * cut, 4 * cut), ROWS)

            if final:
                (two_ref,) = refs

                @pl.when(j == count - 1)
                def _():
                    normal, _ = normalize(middle_ref[...])
                    two_ref[...] = (normal * vec_ref[3:4] + vec_ref[4:5]).astype(LOW)

        outs = [
            (pl.BlockSpec((1, length, 3 * cut), lambda j, _: (j, 0, 0)), out((count, length, 3 * cut), LOW)),
            (pl.BlockSpec((length, cut), lambda j, _: (0, j)), out((length, count * cut), LOW)),
            (pl.BlockSpec((1, 8, length), lambda j, _: (j, 0, 0)), out((count, 8, length), FULL)),
            (pl.BlockSpec((1, fan), lambda j, _: (0, j)), out((1, count * fan), FULL)),
            (fixed((length, width)), out((length, width), FULL)),
        ]
        if first:
            outs.append((fixed((length, width)), out((length, width), LOW)))
            outs.append((fixed((6, width)), out((6, width), FULL)))
        if final:
            outs.append((fixed((length, width)), out((length, width), LOW)))
        return call(
            body,
            (count,),
            [whole(x), whole(mask_row)]
            + self.weight_specs(weights, 4 * cut, lambda j, *_: (j, 0, 0))
            + [whole(a) for a in before or ()],
            [spec for spec, _ in outs],
            [shape for _, shape in outs],
            flops=(8 * length * width * width + 4 * length * length * width) * count // self.tensor,
            size=16 * width * width,
            scalars=self.scalars(),
            room=20,
        )

    def attention_back(self, own, logs, mask_column, branch, weights, start, count, before=None, closing=None):
        cut, length, width = self.cut, self.length, self.width
        base = start % own.shape[0]
        first, final = before is None, closing is not None

        def body(scalars, own_ref, log_ref, mask_ref, branch_ref, *refs):
            w_refs, refs = refs[: self.blocks], refs[self.blocks :]
            if not first:
                (total_in,), refs = refs[:1], refs[1:]
            if final:
                (x_ref, grad_ref, vec_ref), refs = refs[:3], refs[3:]
                part_ref, pair_ref, out_ref, sum_ref, total = refs
            else:
                part_ref, pair_ref, total = refs
            j = pl.program_id(0)

            @pl.when(j == 0)
            def _():
                total[...] = jnp.zeros((length, width), FULL) if first else total_in[...]

            grad_att = dot(branch_ref[...], self.join(w_refs, 3 * cut, 4 * cut)).astype(LOW)
            self.back_heads(own_ref, own_ref, log_ref, mask_ref, grad_att, part_ref, LOW)
            grad = part_ref[0]
            total[...] += dot(grad, self.join(w_refs, 0, 3 * cut), ROWS)
            pair_ref[0] = jnp.sum(grad.astype(FULL), axis=0, keepdims=True)
            if final:

                @pl.when(j == count - 1)
                def _():
                    grad = total[...]
                    normal, scaling = normalize(self.take_all(scalars, x_ref).astype(FULL))
                    result = grad_ref[...] + norm_back(grad, normal, scaling, vec_ref[0:1])
                    self.put_all(scalars, out_ref, result.astype(LOW))
                    sum_ref[0:1] = jnp.sum(grad * normal, axis=0, keepdims=True)
                    sum_ref[1:2] = jnp.sum(grad, axis=0, keepdims=True)

        ins = [
            (own, pl.BlockSpec((1, length, 3 * cut), lambda j, _: (base + j, 0, 0))),
            (logs, pl.BlockSpec((1, 8, length), lambda j, _: (base + j, 0, 0))),
            whole(mask_column),
            whole(branch),
        ]
        ins += self.weight_specs(weights, 4 * cut, lambda j, *_: (base + j, 0, 0))
        ins += [whole(a) for a in ((before,) if before is not None else ()) + (closing or ())]
        outs = [
            (pl.BlockSpec((1, length, 3 * cut), lambda j, _: (j, 0, 0)), out((count, length, 3 * cut), LOW)),
            (pl.BlockSpec((1, 1, 3 * cut), lambda j, _: (j, 0, 0)), out((count, 1, 3 * cut), FULL)),
            (fixed((length, width)), out((length, width), LOW if final else FULL)),
        ]
        if final:
            outs.append((fixed((2, width)), out((2, width), FULL)))
        return call(
            body,
            (count,),
            ins,
            [spec for spec, _ in outs],
            [shape for _, shape in outs],
            [pltpu.VMEM((length, width), FULL)] if final else [],
            flops=(8 * length * width * width + 10 * length * length * width) * count // self.tensor,
            size=32 * width * width,
            scalars=self.scalars(),
            room=24 if final else 18,
        )

    def first_grads(self, normed, branch, grads, attended, smalls=None):
        cut, length, width, depth = self.cut, self.length, self.width, self.depth
        count = attended.shape[1] // cut
        half, lanes = self.blocks // 2, 4 * self.cut
        times = 0 if smalls is None else self.tensor // count
        rows = depth + SMALL_ROWS * times
        smalls = list(smalls or ())

        def body(scalars, normed_ref, branch_ref, att_ref, *refs):
            parts, refs = refs[: len(grads)], refs[len(grads) :]
            kept_ref, sent_ref, turned, turned_two = refs[-4:]
            self.turn(scalars, normed_ref, turned)
            self.turn(scalars, branch_ref, turned_two)
            for j, (ref, k) in enumerate((r, k) for r in parts for k in range(r.shape[0])):
                self.put_halves(kept_ref, sent_ref, j, 0, dot(turned[...], ref[k]).astype(LOW))
                right = att_ref[:, j * cut : (j + 1) * cut]
                self.put_halves(
                    kept_ref, sent_ref, j, 3 * cut, dot(turned_two[...], right).astype(LOW)
                )
            if smalls:
                one_ref, two_ref, row_ref = refs[:3]
                pairs = [(r, k) for r in refs[3 : len(smalls)] for k in range(r.shape[0])]
                six = jnp.concatenate([one_ref[...], two_ref[...]], 0)
                for t, (ref, k) in enumerate(pairs):
                    sums = ref[k]
                    pair = jnp.concatenate([sums[:, :cut], sums[:, 2 * cut :]], 1)
                    at = self.group(scalars, t) * self.fan
                    row = row_ref[:, pl.ds(pl.multiple_of(at, self.fan), self.fan)]
                    at = depth + SMALL_ROWS * (t // count)
                    for o in range(self.blocks):
                        to = (kept_ref, sent_ref)[o // half]
                        to[o % half, t % count, at : at + SMALL_ROWS, :] = small_rows(
                            six[:, o * depth : (o + 1) * depth], pair, row, lanes
                        )

        return call(
            body,
            (1,),
            [whole(a) for a in [normed, branch, attended] + list(grads) + smalls],
            [fixed((half, count, rows, lanes))] * 2,
            [out((half, count, rows, lanes), LOW)] * 2,
            [pltpu.VMEM((width, length), LOW)] * 2,
            flops=8 * length * width * cut * count,
            size=2 * width * lanes * count,
            scalars=self.scalars(),
            room=24,
        )


class Layout:
    def __init__(self, sizes, images):
        self.dp, self.tensor = sizes["dp"], sizes["tensor"]
        self.images = images
        self.groups = self.tensor // images
        self.near = self.dp == 8
        self.me = lax.axis_index("dp")
        self.place = lax.axis_index("tensor")

    def swap(self, array, bit):
        return lax.ppermute(array, "dp", [(k, k ^ bit) for k in range(self.dp)])

    def swap_tensor(self, array, step):
        return lax.ppermute(array, "tensor", [(k, k ^ step) for k in range(self.tensor)])

    def spots(self):
        if not self.near:
            return None
        return jnp.array(ORDER, jnp.int32) ^ self.me.astype(jnp.int32)

    def ordered(self, array):
        if not self.near:
            return array
        return jnp.concatenate(
            [lax.dynamic_slice_in_dim(array, self.me ^ r, 1, 0) for r in ORDER], 0
        )

    def plain(self, array):
        if not self.near:
            return array
        pieces = []
        for block in range(8):
            r = self.me ^ block
            pieces.append(lax.dynamic_slice_in_dim(array, (r & 1) * 4 + (r >> 1), 1, 0))
        return jnp.concatenate(pieces, 0)

    def gather(self, shard):
        line = lax.all_gather(shard, "tensor", axis=0)
        return self.gather_line(line)

    def gather_line(self, line):
        if not self.near:
            return list(lax.all_gather(line, "dp", axis=0))
        half = line.shape[0] // 2
        by_x = self.swap(line, 2)
        by_y = self.swap(line, 4)
        top = self.swap(by_y[:half], 2)
        bottom = self.swap(by_x[half:], 4)
        far = jnp.concatenate([top, bottom], 0)
        mine = [line, by_x, by_y, far]
        return mine + [self.swap(block, 1) for block in mine]

    def scatter(self, kept, sent):
        if not self.near:
            return lax.psum_scatter(jnp.concatenate([kept, sent], 0), "dp", scatter_dimension=0)
        came = self.swap(sent, 1)
        half = kept.shape[1] // 2

        def add(*parts):
            return sum(part.astype(FULL) for part in parts).astype(LOW)

        top = self.swap(add(kept[3, :half], came[3, :half]), 2)
        bottom = self.swap(add(kept[3, half:], came[3, half:]), 4)
        x_block = jnp.concatenate(
            [add(kept[1, :half], came[1, :half]), add(kept[1, half:], came[1, half:], bottom)],
            0,
        )
        y_block = jnp.concatenate(
            [add(kept[2, :half], came[2, :half], top), add(kept[2, half:], came[2, half:])],
            0,
        )
        by_x = self.swap(x_block, 2)
        by_y = self.swap(y_block, 4)
        return add(kept[0], came[0], by_x, by_y)

    def scatter_line(self, total):
        total = lax.psum_scatter(total, "tensor", scatter_dimension=0)
        return total.astype(FULL)

    def scatter_near(self, near, far, lower):
        count = near.shape[0]
        total = near[0, :lower].astype(FULL)
        for step in range(1, count):
            total += self.swap_tensor(near[step, :lower], step).astype(FULL)
        for step in range(count, self.tensor):
            body = self.swap_tensor(far[step - count], step).astype(FULL)
            below = self.swap_tensor(near[step - count, lower:], step).astype(FULL)
            total += jnp.concatenate([body, below], 0)
        return total

    def split(self, array):
        spot = self.place % self.images
        return [
            lax.dynamic_index_in_dim(array, spot ^ step, 1, keepdims=False)
            for step in range(self.images)
        ]

    def to_image(self, blocks):
        came = [
            self.swap_tensor(block, step)
            for step, block in enumerate(blocks)
            if step
        ]
        return jnp.concatenate(blocks[:1] + came, 0)

    def from_image(self, array):
        spot = self.place % self.images
        rows = array.shape[0] // self.images
        blocks = [array[:rows]]
        for step in range(1, self.images):
            part = array[step * rows : (step + 1) * rows]
            blocks.append(self.swap_tensor(part, step))
        return jnp.stack(
            [self.pick(blocks, spot ^ image) for image in range(self.images)], 1
        )

    def pick(self, blocks, index):
        chosen = blocks[0]
        for k in range(1, len(blocks)):
            chosen = jnp.where(index == k, blocks[k], chosen)
        return chosen

    def halves(self, array):
        parts = [array]
        for group in range(1, self.groups):
            parts.append(self.swap_tensor(array, group * self.images))
        return parts[0] if len(parts) == 1 else jnp.concatenate(parts, 1)

    def halves_back(self, array):
        rows = array.shape[1] // self.groups
        total = array[:, :rows]
        for group in range(1, self.groups):
            total = total + self.swap_tensor(array[:, group * rows : (group + 1) * rows], group * self.images)
        return total.astype(LOW)

    def valid_keys(self, key_mask):
        rows = key_mask.shape[1] // self.tensor
        mine = lax.dynamic_index_in_dim(
            key_mask, self.place % self.images, 0, keepdims=False
        )
        return jnp.concatenate(
            [
                lax.dynamic_slice_in_dim(mine, (self.place ^ block) * rows, rows, 0)
                for block in range(self.tensor)
            ]
        )


def shards(
    sizes,
    tokens,
    attn_gain,
    attn_shift,
    qkv_weight,
    query_value_bias,
    proj_weight,
    proj_bias,
    mlp_gain,
    mlp_shift,
    expand_weight,
    expand_bias,
    reduce_weight,
    reduce_bias,
    key_mask,
    cotangent,
):
    lay = Layout(sizes, tokens.shape[1])
    depth = attn_gain.shape[0]
    cut = qkv_weight.shape[2]
    fan = expand_weight.shape[1]
    heads = cut // HD
    slots = query_value_bias.shape[2]
    length = tokens.shape[0] * lay.images
    keys = length * lay.groups
    do = Kernels(lay.dp, depth, lay.tensor, cut, fan, length, keys, lay.spots(), lay.place.astype(jnp.int32))

    token_blocks = lay.split(tokens)
    lanes, count = 4 * cut, expand_bias.size
    six = jnp.stack([attn_gain, attn_shift, proj_bias, mlp_gain, mlp_shift, reduce_bias]).astype(FULL)
    owner = jnp.arange(lay.dp)[:, None] == lay.me
    pair = jnp.where(owner, query_value_bias.astype(FULL)[:, :, None], 0.0).reshape(1, -1)
    row = jnp.where(owner, expand_bias.astype(FULL), 0.0).reshape(1, -1)
    first, turned = do.pack(qkv_weight.transpose(1, 0, 2), proj_weight, reduce_weight, six, pair, row)
    together = lay.groups == 1 and lay.near
    split = lay.tensor // 2
    if together:
        lines = [first] + [lay.swap_tensor(first, k) for k in range(1, lay.tensor)]
        lines[1], token_blocks = lax.optimization_barrier((lines[1], token_blocks))
        near_blocks = lay.gather_line(jnp.stack(lines[:split]))
        far_blocks = lay.gather_line(jnp.stack(lines[split:]))
    else:
        first_blocks = lay.gather(first)
    cot, first = lax.optimization_barrier((cotangent, first))
    cot_blocks = lay.split(cot)
    image = lay.to_image(token_blocks)
    expand_blocks = lay.gather(expand_weight)
    reduce_blocks = lay.gather(turned)
    cot_image = lay.to_image(cot_blocks)
    mask = lay.valid_keys(key_mask)

    if together:
        own, attended, logs, row, middle, normed_one, vectors = do.attention(image, mask[None], near_blocks, split)
        own_two, attended_two, logs_two, row_two, middle, normed_two = do.attention(
            image, mask[None], far_blocks, split, (middle, normed_one, vectors)
        )
        expand_row = jnp.concatenate([row, row_two], 1)
    else:
        normed_one, own, vectors, expand_row = do.project(image, first_blocks)
        full = lay.halves(own)
        attended, logs = do.attend(own, full, mask[None])
        middle, normed_two = do.close_attention(attended, image, vectors, first_blocks)
    hidden, slope = do.expand(normed_two, expand_row, expand_blocks, together)
    block_output = lay.from_image(do.reduce(hidden, middle, vectors, reduce_blocks))

    halves = do.weight_grad(cot_image, [hidden], True)
    reduce_grad = lay.scatter_line(lay.scatter(*halves)).T
    grad_middle, grad_branch, sums, row_grad, grad_before = do.feed_back(
        cot_image, slope, middle, vectors, reduce_blocks, expand_blocks
    )
    halves = do.weight_grad(normed_two, [grad_before], False)
    expand_grad = lay.scatter_line(lay.scatter(*halves))
    if together:
        column = mask[:, None]
        grads, pairs, total = do.attention_back(
            own_two, logs_two, column, grad_branch, far_blocks, split, split
        )
        halves = do.first_grads(normed_one, grad_branch, [grads], attended_two)
        far = lay.scatter(*halves)
        grads, pairs = [], [pairs]
        for start in range(split - 1, 0, -1):
            grad, pair, total = do.attention_back(
                own, logs, column, grad_branch, near_blocks, start, 1, total
            )
            grads, pairs = [grad] + grads, [pair] + pairs
        grad, pair, tokens_grad, sums_one = do.attention_back(
            own, logs, column, grad_branch, near_blocks, 0, 1, total, (image, grad_middle, vectors)
        )
        halves = do.first_grads(
            normed_one, grad_branch, [grad] + grads, attended, [sums_one, sums, row_grad, pair] + pairs
        )
        near = lay.scatter(*halves)
        last = lay.scatter_near(near, far, depth + SMALL_ROWS)
    else:
        grad_query, grad_pair = do.attend_back(
            own, full, logs, mask[:, None], grad_branch, first_blocks, FULL
        )
        grad_pair = lay.halves_back(grad_pair)
        tokens_grad, sums_one, pair_sums = do.project_back(
            grad_query, grad_pair, image, grad_middle, vectors, first_blocks
        )
        qkv_halves = do.weight_grad(normed_one, [grad_query, grad_pair], False)
        proj_halves = do.weight_grad(grad_branch, [attended], False)
        six = jnp.concatenate([sums_one, sums], 0)
        pair_rows = jnp.concatenate([pair_sums[:, 0, :cut], pair_sums[:, 0, 2 * cut :]], 1)
        rows = jnp.stack(
            [
                jnp.stack(
                    [
                        small_rows(
                            six[:, o * depth : (o + 1) * depth],
                            pair_rows[t : t + 1],
                            row_grad[:, t * fan : (t + 1) * fan],
                            lanes,
                        )
                        for t in range(lay.tensor)
                    ]
                )
                for o in range(lay.dp)
            ]
        )
        half = lay.dp // 2
        halves = [
            jnp.concatenate([jnp.concatenate([qkv, proj], 3), small], 2)
            for qkv, proj, small in zip(qkv_halves, proj_halves, (rows[:half], rows[half:]), strict=True)
        ]
        last = lay.scatter_line(lay.scatter(*halves))
    tokens_grad = lay.from_image(tokens_grad)
    vector_grads = last[depth, : 6 * depth].reshape(6, depth)
    pair_grad = last[depth + 1, : 2 * cut].reshape(2, heads, HD)
    pair_grad = lax.dynamic_slice_in_dim(pair_grad, lay.me * slots, slots, 2)
    row_part = lax.dynamic_slice_in_dim(last[depth + 2], lay.me * count, count, 0)
    return (
        block_output,
        tokens_grad,
        vector_grads[0],
        vector_grads[1],
        last[:depth, : 3 * cut].reshape(depth, 3, cut),
        pair_grad,
        last[:depth, 3 * cut :].T,
        vector_grads[2],
        vector_grads[3],
        vector_grads[4],
        expand_grad,
        row_part.reshape(expand_bias.shape),
        reduce_grad,
        vector_grads[5],
    )


def solution(mesh):
    placed = (
        P("tensor", "dp", None),
        P("dp"),
        P("dp"),
        P("dp", None, "tensor"),
        P(None, "tensor", "dp"),
        P("tensor", "dp"),
        P("dp"),
        P("dp"),
        P("dp"),
        P("dp", "tensor"),
        P("tensor", "dp"),
        P("tensor", "dp"),
        P("dp"),
        P("dp", None),
        P("tensor", "dp", None),
    )

    def step(*arrays):
        return shards(dict(mesh.shape), *arrays)

    return jax.shard_map(
        step,
        mesh=mesh,
        in_specs=placed,
        out_specs=(
            P("tensor", "dp", None),
            P("tensor", "dp", None),
            P("dp"),
            P("dp"),
            P("dp", None, "tensor"),
            P(None, "tensor", "dp"),
            P("tensor", "dp"),
            P("dp"),
            P("dp"),
            P("dp"),
            P("dp", "tensor"),
            P("tensor", "dp"),
            P("tensor", "dp"),
            P("dp"),
        ),
        check_vma=False,
    )
```
